128 devices in a mesh: sample: 8 (over y_lo, z), mp: 16 (over x, y_hi, core).
Axes of the slice: x: 4, y: 4 (y_hi: 2, y_lo: 2; y = y_hi * 2 + y_lo), z: 4, core: 2. Of those that a mesh axis runs over, the one named last changes fastest.
Arguments:
- volumes: bfloat16 [64, 8, 4096], P('mp', 'sample'), may hold values from -6 to 6
- w_first: bfloat16 [128, 1728], P('mp'), may hold values from -0.15625 to 0.15625
- w_second: bfloat16 [256, 3456], P('mp'), may hold values from -0.109375 to 0.109375
- cotangent: bfloat16 [256, 8, 4096], P('mp', 'sample'), may hold values from -6 to 6
Outputs:
- features: bfloat16 [256, 8, 4096], P('mp', 'sample')
- input_grad: bfloat16 [64, 8, 4096], P('mp', 'sample')
- grad_first: float32 [128, 1728], P('mp')
- grad_second: float32 [256, 3456], P('mp')
The draws below stay inside these ranges and needn't reach their ends.
All inputs are finite; a program needn't handle non-finite values.
Results may differ from the reference program's by a relative error of at most 0.024.
Values may be sent and summed in bfloat16 or wider, within the bound.
A program may use at most 64 MiB of HBM per device.

```python
import math
import jax
import jax.numpy as jnp
from jax import lax

C0 = 64
C1 = 128
C2 = 256
SIDE = 16
DEPTH = 16
CELLS = 4096
BATCH = 8


def steps_of(own_key, extent, split, low, high):
    factor_of = 1.0
    for axis_at, shards_of in split:
        draws = jax.random.uniform(jax.random.fold_in(jax.random.fold_in(own_key, 6), axis_at), (shards_of,), jnp.float32, low / len(split), high / len(split))
        factor_of = factor_of * jnp.repeat(jnp.exp(draws), extent[axis_at] // shards_of).reshape((-1,) + (1,) * (len(extent) - 1 - axis_at))
    return factor_of


def centred(rng, dims, width, most, shards=(), kind=jnp.bfloat16):
    values = width * jax.random.normal(rng, dims, jnp.float32)
    if shards:
        values = values * steps_of(rng, dims, shards, -0.22, 0.18)
    return jnp.clip(values, -most, most).astype(kind)


def setup_inputs(seed: int = 0) -> dict:
    arg_keys = jax.random.split(jax.random.key(seed), 5)
    return {
        "volumes": centred(arg_keys[0], (C0, BATCH, CELLS), 1.0, 6.0, ((0, 16), (1, 8))),
        "w_first": centred(arg_keys[1], (C1, 27 * C0), (27 * C0) ** -0.5, 0.15625, ((0, 16),)),
        "w_second": centred(arg_keys[2], (C2, 27 * C1), (27 * C1) ** -0.5, 0.109375, ((0, 16),)),
        "cotangent": centred(arg_keys[3], (C2, BATCH, CELLS), 1.0, 6.0, ((0, 16), (1, 8))),
    }


def to_grid(array_in):
    return array_in.reshape(array_in.shape[0], array_in.shape[1], DEPTH, SIDE, SIDE)

def conv_forward(inputs, weights):
    filters = weights.shape[0]
    kernel = weights.astype(jnp.float32).reshape(filters, 3, 3, 3, inputs.shape[0])
    output = lax.conv_general_dilated(to_grid(inputs.astype(jnp.float32)), kernel, (1, 1, 1), ((1, 1), (1, 1), (1, 1)), dimension_numbers=('CNDHW', 'ODHWI', 'CNDHW'), precision=lax.Precision.HIGHEST)
    return output.reshape(filters, inputs.shape[1], -1)

def conv_data(deltas, weights, channels):
    kernel = weights.astype(jnp.float32).reshape(weights.shape[0], 3, 3, 3, channels)[:, ::-1, ::-1, ::-1, :]
    output = lax.conv_general_dilated(to_grid(deltas.astype(jnp.float32)), kernel, (1, 1, 1), ((1, 1), (1, 1), (1, 1)), dimension_numbers=('CNDHW', 'IDHWO', 'CNDHW'), precision=lax.Precision.HIGHEST)
    return output.reshape(channels, deltas.shape[1], -1)

def conv_weight(inputs, deltas):
    output = lax.conv_general_dilated(to_grid(inputs.astype(jnp.float32)), to_grid(deltas.astype(jnp.float32)), (1, 1, 1), ((1, 1), (1, 1), (1, 1)), dimension_numbers=('NCDHW', 'OIDHW', 'NCDHW'), precision=lax.Precision.HIGHEST)
    return jnp.transpose(output, (1, 2, 3, 4, 0)).reshape(deltas.shape[0], -1)

def silu_slope(values):
    sigmoid_v = jax.nn.sigmoid(values)
    return sigmoid_v * (1.0 + values * (1.0 - sigmoid_v))

def reference(volumes, w_first, w_second, cotangent):
    pre_first = conv_forward(volumes, w_first)
    hidden = jax.nn.silu(pre_first).astype(jnp.bfloat16)
    pre_second = conv_forward(hidden, w_second)
    features = jax.nn.silu(pre_second).astype(jnp.bfloat16)
    delta_second = (cotangent.astype(jnp.float32) * silu_slope(pre_second)).astype(jnp.bfloat16)
    grad_hidden = conv_data(delta_second, w_second, hidden.shape[0])
    delta_first = (grad_hidden * silu_slope(pre_first)).astype(jnp.bfloat16)
    input_grad = conv_data(delta_first, w_first, volumes.shape[0]).astype(jnp.bfloat16)
    grad_scale = 1.0 / math.sqrt(volumes.shape[1] * volumes.shape[2])
    grad_second = conv_weight(hidden, delta_second) * grad_scale
    grad_first = conv_weight(volumes, delta_first) * grad_scale
    return (features, input_grad, grad_first, grad_second)
```

```python
import functools
import math

import jax
import jax.numpy as jnp
from jax import lax
from jax.experimental import pallas as pl
from jax.experimental.pallas import tpu as pltpu
from jax.sharding import PartitionSpec as P

MESH = pl.DeviceIdType.MESH
F32 = jnp.float32
BF16 = jnp.bfloat16
PLANE = 256
OWN = 8
HALF = OWN * PLANE
WIDE1 = HALF + 2 * PLANE
WIDE2 = HALF + 4 * PLANE


def at(start, size, unit):
    return pl.ds(pl.multiple_of(start, unit), size)


def plane_at(index, planes=1):
    return at(index * PLANE, planes * PLANE, PLANE)


def place(rows, lanes):
    return lax.broadcasted_iota(jnp.int32, (rows, lanes), 1)


def shifted_x(value, step):
    rows, lanes = value.shape
    x = place(rows, lanes) % 16
    if step > 0:
        return jnp.where(x < 15, pltpu.roll(value, lanes - 1, 1), 0.0)
    return jnp.where(x > 0, pltpu.roll(value, 1, 1), 0.0)


def shifted_y(value, step):
    rows, lanes = value.shape
    cell = place(rows, lanes)
    if step > 0:
        return jnp.where(cell < PLANE - 16, pltpu.roll(value, lanes - 16, 1), 0.0)
    return jnp.where(cell >= 16, pltpu.roll(value, 16, 1), 0.0)


def sigmoid(v):
    return 1.0 / (1.0 + jnp.exp(-v))


def slope(v):
    s = sigmoid(v)
    return s * (1.0 + v * (1.0 - s))


def mm(a, b, ca, cb):
    return lax.dot_general(a, b, (((ca,), (cb,)), ((), ())), preferred_element_type=F32)


def conv_plane(y_ref, rows, p):
    sums = []
    for dy in range(3):
        total = None
        for dz in range(3):
            k = 3 * dz + dy
            part = y_ref[rows * k : rows * (k + 1), plane_at(p + dz)]
            total = part if total is None else total + part
        sums.append(total)
    return sums[1] + shifted_y(sums[0], -1) + shifted_y(sums[2], 1)


def kernel(
    scale, vol, w1, w2, cot, feat, ig_out, g1_out, g2_out,
    vrecv, wb1, wb2, cb, w1s, w2s, vf, v3, y1, pre1, h, h3, y2, fb, fr, dlb, halo2, e2,
    ghb, ghr, d1b, halo1, e1, igb, igr, gsf, gsx, gsr, gp, gpr, gq, g1f, g1x, g1r, g1t, g1b, g1q,
    loc, sib_s, sib_r, vs, vr, hs, hr, gs, gr, is_, ir, ps, pr, qs, qr, g1s, g1rr,
):
    s = lax.axis_index("sample")
    m = lax.axis_index("mp")
    core = m % 2
    chip = m // 2
    sib = chip * 2 + (1 - core)
    waits = []

    def send(src, dst, ssem, rsem, sample, mp):
        c = pltpu.make_async_remote_copy(
            src_ref=src, dst_ref=dst, send_sem=ssem, recv_sem=rsem,
            device_id=(sample, mp), device_id_type=MESH,
        )
        c.start()
        waits.append(c)
        return c

    barrier = pltpu.get_barrier_semaphore()
    for r in range(1, 16):
        pl.semaphore_signal(barrier, inc=1, device_id=(s, (m + r) % 16), device_id_type=MESH)
    for r in range(1, 8):
        pl.semaphore_signal(barrier, inc=1, device_id=((s + r) % 8, m), device_id_type=MESH)

    half = at(core * HALF, HALF, HALF)
    other = at((1 - core) * HALF, HALF, HALF)
    local = [
        pltpu.make_async_copy(vol.at[:, at(core * 1536, WIDE1, PLANE)], vrecv.at[m], loc.at[0]),
        pltpu.make_async_copy(w1, wb1.at[core], loc.at[1]),
        pltpu.make_async_copy(w2, wb2.at[core], loc.at[2]),
        pltpu.make_async_copy(cot.at[:, half], cb.at[core], loc.at[3]),
    ]
    for c in local:
        c.start()
    pl.semaphore_wait(barrier, 22)

    vol_copies = []
    for r in range(1, 16):
        to = (m + r) % 16
        src = vol.at[:, at((to % 2) * 1536, WIDE1, PLANE)]
        vol_copies.append(send(src, vrecv.at[m], vs.at[r - 1], vr.at[r - 1], s, to))
    w1_copy = send(w1, wb1.at[core], sib_s.at[0], sib_r.at[0], s, sib)
    w2_copy = send(w2, wb2.at[core], sib_s.at[1], sib_r.at[1], s, sib)
    cot_copy = send(cot.at[:, other], cb.at[core], sib_s.at[2], sib_r.at[2], s, sib)

    local[1].wait()
    w1_copy.wait_recv()
    w1_all = jnp.concatenate([wb1[0].astype(F32), wb1[1].astype(F32)], axis=0)
    for k in range(9):
        w1s[16 * k : 16 * k + 16, :] = w1_all[:, 192 * k : 192 * k + 192].astype(BF16)
    local[2].wait()
    w2_copy.wait_recv()
    for k in range(9):
        for c in range(2):
            w2s[32 * k + 16 * c : 32 * k + 16 * c + 16, :] = wb2[c, :, 384 * k : 384 * k + 384]
    gp[27:32] = jnp.zeros((5, 16, 128), BF16)
    vf[:, at(core * WIDE1, 2 * PLANE, PLANE)] = jnp.zeros((64, 2 * PLANE), F32)
    local[0].wait()
    for c in vol_copies:
        c.wait_recv()
    for i in range(16):
        vf[4 * i : 4 * i + 4, at((1 - core) * 2 * PLANE, WIDE1, PLANE)] = vrecv[i].astype(F32)

    def stack_v(p, _):
        value = vf[:, plane_at(p)]
        for dx in range(3):
            part = value if dx == 1 else shifted_x(value, dx - 1)
            v3[64 * dx : 64 * dx + 64, plane_at(p)] = part.astype(BF16)
        y1[:, plane_at(p)] = mm(w1s[...], v3[:, plane_at(p)], 1, 0)
        return 0

    lax.fori_loop(0, 12, stack_v, 0)

    rows16 = at(chip * 16, 16, 16)

    def first(p, _):
        value = conv_plane(y1, 16, p)
        pre1[:, plane_at(p)] = value
        z = core * OWN + p - 1
        inside = jnp.logical_and(z >= 0, z < 16)
        hidden = jnp.where(inside, value * sigmoid(value), 0.0)
        h[rows16, plane_at(p)] = hidden.astype(BF16)
        return 0

    lax.fori_loop(0, 10, first, 0)

    h_copies = []
    for r in range(1, 8):
        to = ((chip + r) % 8) * 2 + core
        h_copies.append(send(h.at[rows16], h.at[rows16], hs.at[r - 1], hr.at[r - 1], s, to))
    local[3].wait()
    cot_copy.wait_recv()
    for c in h_copies:
        c.wait_recv()

    def stack_h(p, _):
        value = h[:, plane_at(p)].astype(F32)
        for dx in range(3):
            part = value if dx == 1 else shifted_x(value, dx - 1)
            h3[128 * dx : 128 * dx + 128, plane_at(p)] = part.astype(BF16)
        y2[:, plane_at(p)] = mm(w2s[...], h3[:, plane_at(p)], 1, 0)
        return 0

    lax.fori_loop(0, 10, stack_h, 0)

    def second(p, _):
        value = conv_plane(y2, 32, p)
        sg = sigmoid(value)
        out = (value * sg).astype(BF16)
        fb[0, :, plane_at(p)] = out[:16]
        fb[1, :, plane_at(p)] = out[16:]
        cots = jnp.concatenate([cb[0, :, plane_at(p)], cb[1, :, plane_at(p)]], axis=0)
        delta = cots.astype(F32) * (sg * (1.0 + value * (1.0 - sg)))
        dlb[:, plane_at(p + 1)] = delta.astype(BF16)
        return 0

    lax.fori_loop(0, OWN, second, 0)

    edge = plane_at(OWN - (OWN - 1) * core)
    halo2_copy = send(dlb.at[:, edge], halo2, sib_s.at[3], sib_r.at[3], s, sib)
    feat_copy = send(fb.at[1 - core], fr, sib_s.at[4], sib_r.at[4], s, sib)

    def spread(src, dst, rows):
        def body(p, _):
            value = src[:, plane_at(p)].astype(F32)
            dst[0:rows, plane_at(p)] = shifted_y(value, 1).astype(BF16)
            dst[rows : 2 * rows, plane_at(p)] = value.astype(BF16)
            dst[2 * rows : 3 * rows, plane_at(p)] = shifted_y(value, -1).astype(BF16)
            return 0

        return body

    def halos(src, dst, rows, received):
        value = received[...].astype(F32)
        for p, mine in ((0, core == 1), (OWN + 1, core == 0)):
            src[:, PLANE * p : PLANE * (p + 1)] = jnp.where(mine, value, 0.0).astype(BF16)
            spread(src, dst, rows)(p, 0)

    lax.fori_loop(1, OWN + 1, spread(dlb, e2, 32), 0)
    halo2_copy.wait_recv()
    halos(dlb, e2, 32, halo2)

    def around(e, p):
        return jnp.concatenate([e[:, plane_at(p + 2 - dz)] for dz in range(3)], axis=0)

    def collect(z, rows):
        return z[rows : 2 * rows] + shifted_x(z[:rows], 1) + shifted_x(z[2 * rows :], -1)

    def hidden_grad(p, _):
        z = mm(w2s[...], around(e2, p), 0, 0)
        ghb[:, plane_at(p)] = collect(z, 128).astype(BF16)
        return 0

    lax.fori_loop(0, OWN, hidden_grad, 0)

    gh_copies = []
    for r in range(1, 8):
        to = (chip + r) % 8
        src = ghb.at[at(to * 16, 16, 16)]
        gh_copies.append(send(src, ghr.at[r - 1], gs.at[r - 1], gr.at[r - 1], s, to * 2 + core))

    for dz in range(3):
        part = mm(e2[:, PLANE * (2 - dz) : PLANE * (2 - dz) + HALF], h3[:, PLANE : PLANE + HALF], 1, 1)
        for dy in range(3):
            gsf[3 * dz + dy] = part[32 * dy : 32 * dy + 32]
    mine16 = at(core * 16, 16, 16)
    gsx[...] = gsf[:, at((1 - core) * 16, 16, 16), :].astype(BF16)
    gs_copy = send(gsx, gsr, sib_s.at[5], sib_r.at[5], s, sib)
    feat_copy.wait_recv()
    feat[:, half] = fb[core]
    feat[:, other] = fr[...]
    gs_copy.wait_recv()
    for k in range(9):
        part = (gsf[k, mine16, :] + gsr[k].astype(F32)).astype(BF16)
        for dx in range(3):
            gp[3 * k + dx] = part[:, 128 * dx : 128 * dx + 128]
    gp_copies = []
    for r in range(1, 8):
        to = (s + r) % 8
        gp_copies.append(send(gp.at[pl.ds(4 * to, 4)], gpr.at[r - 1], ps.at[r - 1], pr.at[r - 1], to, m))

    for c in gh_copies:
        c.wait_recv()

    def delta_first(p, _):
        total = ghb[rows16, plane_at(p)].astype(F32)
        for r in range(7):
            total += ghr[r, :, plane_at(p)].astype(F32)
        d1b[:, plane_at(p + 1)] = (total * slope(pre1[:, plane_at(p + 1)])).astype(BF16)
        return 0

    lax.fori_loop(0, OWN, delta_first, 0)
    halo1_copy = send(d1b.at[:, edge], halo1, sib_s.at[6], sib_r.at[6], s, sib)
    lax.fori_loop(1, OWN + 1, spread(d1b, e1, 16), 0)
    halo1_copy.wait_recv()
    halos(d1b, e1, 16, halo1)

    def input_grad(p, _):
        z = mm(w1s[...], around(e1, p), 0, 0)
        value = collect(z, 64)
        for i in range(16):
            igb[i, :, plane_at(p)] = value[4 * i : 4 * i + 4].astype(BF16)
        return 0

    lax.fori_loop(0, OWN, input_grad, 0)

    ig_copies = []
    for r in range(1, 16):
        to = (m + r) % 16
        ig_copies.append(send(igb.at[to], igr.at[r - 1], is_.at[r - 1], ir.at[r - 1], s, to))

    for dz in range(3):
        lanes = slice(PLANE * (2 - dz), PLANE * (2 - dz) + HALF)
        part = mm(e1[:, lanes], v3[:, 2 * PLANE : 2 * PLANE + HALF], 1, 1)
        for dy in range(3):
            g1f[3 * dz + dy] = part[16 * dy : 16 * dy + 16]
    g1x[...] = g1f[:, at((1 - core) * 8, 8, 8), :].astype(BF16)
    g1_copy = send(g1x, g1r, sib_s.at[7], sib_r.at[7], s, sib)

    for c in gp_copies:
        c.wait_recv()
    quarter = pl.ds(4 * s, 4)
    total = gp[quarter].astype(F32)
    for r in range(7):
        total += gpr[r].astype(F32)
    gq[quarter] = (total * scale).astype(BF16)
    gq_copies = []
    for r in range(1, 8):
        to = (s + r) % 8
        gq_copies.append(send(gq.at[quarter], gq.at[quarter], qs.at[r - 1], qr.at[r - 1], to, m))

    g1_copy.wait_recv()
    mine8 = at(core * 8, 8, 8)
    for k in range(9):
        g1t[:, 192 * k : 192 * k + 192] = g1f[k, mine8, :] + g1r[k].astype(F32)
    g1b[...] = g1t[...].astype(BF16)
    g1_copies = []
    for r in range(1, 8):
        to = (s + r) % 8
        g1_copies.append(send(g1b, g1q.at[r - 1], g1s.at[r - 1], g1rr.at[r - 1], to, m))

    for c in ig_copies:
        c.wait_recv()
    same = igb[m].astype(F32)
    for r in range(2, 16, 2):
        same += igr[r - 1].astype(F32)
    ig_out[:, half] = same.astype(BF16)
    across = igr[0].astype(F32)
    for r in range(3, 16, 2):
        across += igr[r - 1].astype(F32)
    ig_out[:, other] = across.astype(BF16)

    for c in gq_copies:
        c.wait_recv()
    for t in range(27):
        g2_out[:, 128 * t : 128 * t + 128] = gq[t].astype(F32)
    for c in g1_copies:
        c.wait_recv()
    total = g1t[...]
    for r in range(7):
        total += g1q[r].astype(F32)
    g1_out[...] = total * scale

    for c in waits:
        c.wait_send()


def local_step(volumes, w_first, w_second, cotangent):
    cells = 2 * HALF
    scale = 1.0 / math.sqrt(lax.axis_size("sample") * volumes.shape[1] * cells)
    V = pltpu.VMEM
    dma = pltpu.SemaphoreType.DMA
    scratch = [
        V((16, 4, WIDE1), BF16), V((2, 8, 1728), BF16), V((2, 16, 3456), BF16), V((2, 16, HALF), BF16),
        V((144, 192), BF16), V((288, 384), BF16), V((64, WIDE2), F32), V((192, WIDE2), BF16),
        V((144, WIDE2), F32), V((16, WIDE1), F32), V((128, WIDE1), BF16), V((384, WIDE1), BF16),
        V((288, WIDE1), F32), V((2, 16, HALF), BF16), V((16, HALF), BF16), V((32, WIDE1), BF16),
        V((32, PLANE), BF16), V((96, WIDE1), BF16),
        V((128, HALF), BF16), V((7, 16, HALF), BF16), V((16, WIDE1), BF16), V((16, PLANE), BF16),
        V((48, WIDE1), BF16), V((16, 4, HALF), BF16), V((15, 4, HALF), BF16),
        V((9, 32, 384), F32), V((9, 16, 384), BF16), V((9, 16, 384), BF16),
        V((32, 16, 128), BF16), V((7, 4, 16, 128), BF16), V((32, 16, 128), BF16),
        V((9, 16, 192), F32), V((9, 8, 192), BF16), V((9, 8, 192), BF16),
        V((8, 1728), F32), V((8, 1728), BF16), V((7, 8, 1728), BF16),
        dma((4,)), dma((8,)), dma((8,)), dma((15,)), dma((15,)), dma((7,)), dma((7,)),
        dma((7,)), dma((7,)), dma((15,)), dma((15,)), dma((7,)), dma((7,)), dma((7,)), dma((7,)),
        dma((7,)), dma((7,)),
    ]
    any_space = pl.BlockSpec(memory_space=pl.ANY)
    vmem = pl.BlockSpec(memory_space=pltpu.VMEM)
    feat, ig, g1, g2 = pl.pallas_call(
        functools.partial(kernel, scale),
        out_shape=(
            jax.ShapeDtypeStruct((16, cells), BF16),
            jax.ShapeDtypeStruct((4, cells), BF16),
            jax.ShapeDtypeStruct((8, 1728), F32),
            jax.ShapeDtypeStruct((16, 3456), F32),
        ),
        in_specs=[any_space] * 4,
        out_specs=(vmem,) * 4,
        scratch_shapes=scratch,
        compiler_params=pltpu.CompilerParams(
            collective_id=0, has_side_effects=True, vmem_limit_bytes=60 * 1024 * 1024
        ),
    )(volumes.reshape(4, cells), w_first, w_second, cotangent.reshape(16, cells))
    return feat.reshape(16, 1, cells), ig.reshape(4, 1, cells), g1, g2


def solution(mesh):
    return jax.shard_map(
        local_step,
        mesh=mesh,
        in_specs=(P("mp", "sample", None), P("mp", None), P("mp", None), P("mp", "sample", None)),
        out_specs=(P("mp", "sample", None), P("mp", "sample", None), P("mp", None), P("mp", None)),
        check_vma=False,
    )
```

```python
import functools
import math

import jax
import jax.numpy as jnp
from jax import lax
from jax.experimental import pallas as pl
from jax.experimental.pallas import tpu as pltpu
from jax.sharding import PartitionSpec as P

MESH = pl.DeviceIdType.MESH
F32 = jnp.float32
BF16 = jnp.bfloat16
PLANE = 256
OWN = 4
SLAB = OWN * PLANE
WIDE1 = SLAB + 2 * PLANE
WIDE2 = SLAB + 4 * PLANE


def at(start, size, unit):
    return pl.ds(pl.multiple_of(start, unit), size)


def plane_at(index, planes=1):
    return at(index * PLANE, planes * PLANE, PLANE)


def place(rows, lanes):
    return lax.broadcasted_iota(jnp.int32, (rows, lanes), 1)


def shifted_x(value, step):
    rows, lanes = value.shape
    x = place(rows, lanes) % 16
    if step > 0:
        return jnp.where(x < 15, pltpu.roll(value, lanes - 1, 1), 0.0)
    return jnp.where(x > 0, pltpu.roll(value, 1, 1), 0.0)


def shifted_y(value, step):
    rows, lanes = value.shape
    cell = place(rows, lanes)
    if step > 0:
        return jnp.where(cell < PLANE - 16, pltpu.roll(value, lanes - 16, 1), 0.0)
    return jnp.where(cell >= 16, pltpu.roll(value, 16, 1), 0.0)


def sigmoid(v):
    return 1.0 / (1.0 + jnp.exp(-v))


def slope(v):
    s = sigmoid(v)
    return s * (1.0 + v * (1.0 - s))


def mm(a, b, ca, cb):
    return lax.dot_general(a, b, (((ca,), (cb,)), ((), ())), preferred_element_type=F32)


def conv_plane(y_ref, rows, p):
    sums = []
    for dy in range(3):
        total = None
        for dz in range(3):
            k = 3 * dz + dy
            part = y_ref[rows * k : rows * (k + 1), plane_at(p + dz)]
            total = part if total is None else total + part
        sums.append(total)
    return sums[1] + shifted_y(sums[0], -1) + shifted_y(sums[2], 1)


def kernel(
    scale, vol, w1, w2, cot, feat, ig_out, g1_out, gq,
    vrecv, wb1, wb2, cb, w1s, w2s, vf, v3, y1, pre1, h, h3, y2, fb, fr, e2,
    ghb, ghr, ghe, e1, igb, igr, gsf, gsx, gsr, gp, gpr, g1f, g1x, g1r, g1t, g1b, g1q,
    loc, vs, vr, w1ss, w1sr, w2ss, w2sr, cs, cr, hs, hr, fs, frs, gs, gr, es, er, xs, xr,
    is_, ir, x1s, x1r, ps, pr, qs, qr, g1s, g1rr,
):
    s = lax.axis_index("sample")
    m = lax.axis_index("mp")
    col = m // 4
    q = m % 4
    waits = []

    def send(src, dst, ssem, rsem, sample, mp):
        c = pltpu.make_async_remote_copy(
            src_ref=src, dst_ref=dst, send_sem=ssem, recv_sem=rsem,
            device_id=(sample, mp), device_id_type=MESH,
        )
        c.start()
        waits.append(c)
        return c

    def slab_peer(r):
        return col * 4 + (q + r) % 4

    def col_peer(r):
        return ((col + r) % 4) * 4 + q

    def to_slabs(source, dst, ssem, rsem):
        return [
            send(source((q + r) % 4, r), dst(r), ssem.at[r - 1], rsem.at[r - 1], s, slab_peer(r))
            for r in (2, 1, 3)
        ]

    barrier = pltpu.get_barrier_semaphore()
    for r in range(1, 16):
        pl.semaphore_signal(barrier, inc=1, device_id=(s, (m + r) % 16), device_id_type=MESH)
    for r in range(1, 8):
        pl.semaphore_signal(barrier, inc=1, device_id=((s + r) % 8, m), device_id_type=MESH)

    def vol_part(slab):
        first = jnp.clip(slab * OWN - 2, 0, 8)
        return vol.at[:, plane_at(first, OWN + 4)]

    def slab_at(slab):
        return at(slab * SLAB, SLAB, SLAB)

    local = [
        pltpu.make_async_copy(vol_part(q), vrecv.at[m], loc.at[0]),
        pltpu.make_async_copy(w1, wb1.at[q], loc.at[1]),
        pltpu.make_async_copy(w2, wb2.at[q], loc.at[2]),
        pltpu.make_async_copy(cot.at[:, slab_at(q)], cb.at[q], loc.at[3]),
    ]
    for c in local:
        c.start()
    gp[27:32] = jnp.zeros((5, 16, 128), BF16)
    vf[...] = jnp.zeros(vf.shape, F32)
    pl.semaphore_wait(barrier, 22)

    vol_copies = []
    for r in (10, 8, 11, 9, 6, 14, 2, 7, 5, 15, 13, 4, 12, 3, 1):
        to = (m + r) % 16
        vol_copies.append(send(vol_part(to % 4), vrecv.at[m], vs.at[r - 1], vr.at[r - 1], s, to))
    w1_copies = to_slabs(lambda slab, r: w1, lambda r: wb1.at[q], w1ss, w1sr)

    local[1].wait()
    for c in w1_copies:
        c.wait_recv()
    w1_all = jnp.concatenate([wb1[i].astype(F32) for i in range(4)], axis=0)
    for k in range(9):
        w1s[32 * k : 32 * k + 32, :] = w1_all[:, 192 * k : 192 * k + 192].astype(BF16)
    local[0].wait()
    for c in vol_copies:
        c.wait_recv()
    core_peer = col * 4 + q + 1 - 2 * (q % 2)
    w2_core = send(w2, wb2.at[q], w2ss.at[0], w2sr.at[0], s, core_peer)
    w2_far = send(w2, wb2.at[q], w2ss.at[1], w2sr.at[1], s, slab_peer(2))
    cot_copies = to_slabs(lambda slab, r: cot.at[:, slab_at(slab)], lambda r: cb.at[q], cs, cr)
    first = jnp.clip(q * OWN - 2, 0, 8) - q * OWN + 4
    for i in range(16):
        vf[4 * i : 4 * i + 4, plane_at(first, OWN + 4)] = vrecv[i].astype(F32)

    for p in range(8):
        lanes = slice(PLANE * p, PLANE * (p + 1))
        value = vf[:, PLANE * (p + 2) : PLANE * (p + 3)]
        for dx in range(3):
            part = value if dx == 1 else shifted_x(value, dx - 1)
            v3[64 * dx : 64 * dx + 64, lanes] = part.astype(BF16)
        y1[:, lanes] = mm(w1s[...], v3[:, lanes], 1, 0)

    rows32 = at(col * 32, 32, 32)
    h_copies = []
    for half in range(2):
        for p in range(3 * half, 3 * half + 3):
            lanes = slice(PLANE * p, PLANE * (p + 1))
            value = conv_plane(y1, 32, p)
            pre1[:, lanes] = value
            z = q * OWN + p - 1
            inside = jnp.logical_and(z >= 0, z < 16)
            hidden = jnp.where(inside, value * sigmoid(value), 0.0)
            h[rows32, lanes] = hidden.astype(BF16)
        part = h.at[rows32, 3 * half * PLANE : 3 * (half + 1) * PLANE]
        for r in (2, 1, 3):
            i = 3 * half + r - 1
            h_copies.append(send(part, part, hs.at[i], hr.at[i], s, col_peer(r)))

    far = wb2.at[(q + 2) % 4]
    w2_far.wait_recv()
    w2_pass = send(far, far, w2ss.at[2], w2sr.at[2], s, core_peer)
    local[2].wait()
    w2_core.wait_recv()
    w2_pass.wait_recv()
    for k in range(9):
        for c in range(4):
            w2s[64 * k + 16 * c : 64 * k + 16 * c + 16, :] = wb2[c, :, 384 * k : 384 * k + 384]
    for half in range(2):
        for c in h_copies[3 * half : 3 * half + 3]:
            c.wait_recv()
        for p in range(3 * half, 3 * half + 3):
            lanes = slice(PLANE * p, PLANE * (p + 1))
            value = h[:, lanes].astype(F32)
            for dx in range(3):
                part = value if dx == 1 else shifted_x(value, dx - 1)
                h3[128 * dx : 128 * dx + 128, lanes] = part.astype(BF16)
            y2[:, lanes] = mm(w2s[...], h3[:, lanes], 1, 0)

    def spread(value, dst, rows, p):
        lanes = slice(PLANE * p, PLANE * (p + 1))
        value = value.astype(BF16).astype(F32)
        dst[0:rows, lanes] = shifted_y(value, 1).astype(BF16)
        dst[rows : 2 * rows, lanes] = value.astype(BF16)
        dst[2 * rows : 3 * rows, lanes] = shifted_y(value, -1).astype(BF16)

    def transposed(w, e, i, rows):
        taps = [dz for dz in range(3) if 0 <= i - dz < OWN]
        parts = [e[:, PLANE * (i - dz) : PLANE * (i - dz + 1)] for dz in taps]
        size = e.shape[0]
        z = mm(w[size * taps[0] : size * (taps[-1] + 1), :], jnp.concatenate(parts, axis=0), 0, 0)
        return z[rows : 2 * rows] + shifted_x(z[:rows], 1) + shifted_x(z[2 * rows :], -1)

    local[3].wait()
    for c in cot_copies:
        c.wait_recv()
    for p in range(OWN):
        lanes = slice(PLANE * p, PLANE * (p + 1))
        value = conv_plane(y2, 64, p)
        sg = sigmoid(value)
        out = (value * sg).astype(BF16)
        for i in range(4):
            fb[i, :, lanes] = out[16 * i : 16 * i + 16]
        cots = jnp.concatenate([cb[i, :, lanes] for i in range(4)], axis=0)
        spread(cots.astype(F32) * (sg * (1.0 + value * (1.0 - sg))), e2, 64, p)

    edge_copies = []
    for side, i in enumerate((0, OWN + 1)):
        lanes = slice(PLANE * i, PLANE * (i + 1))
        ghb[:, lanes] = transposed(w2s, e2, i, 128).astype(BF16)
        for r in (2, 1, 3, 0):
            to = (col + r) % 4
            n = 4 * side + r
            src = ghb.at[at(to * 32, 32, 32), lanes]
            there = to * 4 + (q + 3 - 2 * side) % 4
            edge_copies.append(send(src, ghe.at[n], es.at[n], er.at[n], s, there))
    gh_copies = []
    for half in range(2):
        for i in (1 + 2 * half, 2 + 2 * half):
            lanes = slice(PLANE * i, PLANE * (i + 1))
            ghb[:, lanes] = transposed(w2s, e2, i, 128).astype(BF16)
        lanes = slice(PLANE * (1 + 2 * half), PLANE * (3 + 2 * half))
        for r in (2, 1, 3):
            to = (col + r) % 4
            n = 3 * half + r - 1
            src = ghb.at[at(to * 32, 32, 32), lanes]
            gh_copies.append(send(src, ghr.at[n], gs.at[n], gr.at[n], s, col_peer(r)))

    for dz in range(3):
        part = mm(e2[...], h3[:, PLANE * dz : PLANE * dz + SLAB], 1, 1)
        for dy in range(3):
            gsf[3 * dz + dy] = part[64 * dy : 64 * dy + 64]
    for r in range(1, 4):
        gsx[r - 1] = gsf[:, at(((q + r) % 4) * 16, 16, 16), :].astype(BF16)
    gs_copies = to_slabs(lambda slab, r: gsx.at[r - 1], lambda r: gsr.at[r - 1], xs, xr)
    feat_copies = to_slabs(lambda slab, r: fb.at[slab], lambda r: fr.at[q], fs, frs)

    for c in gh_copies + edge_copies:
        c.wait_recv()
    for p in range(OWN):
        lanes = slice(PLANE * (p + 1), PLANE * (p + 2))
        total = ghb[rows32, lanes].astype(F32)
        part = slice(PLANE * (p % 2), PLANE * (p % 2 + 1))
        for r in range(3):
            total += ghr[3 * (p // 2) + r, :, part].astype(F32)
        for edge, side, inside in ((0, 1, q > 0), (OWN - 1, 0, q < 3)):
            if p == edge:
                more = ghe[4 * side].astype(F32)
                for r in range(1, 4):
                    more += ghe[4 * side + r].astype(F32)
                total += jnp.where(inside, more, 0.0)
        spread(total * slope(pre1[:, lanes]), e1, 32, p)

    for dz in range(3):
        part = mm(e1[...], v3[:, PLANE * (1 + dz) : PLANE * (1 + dz) + SLAB], 1, 1)
        for dy in range(3):
            g1f[3 * dz + dy] = part[32 * dy : 32 * dy + 32]
    for r in range(1, 4):
        g1x[r - 1] = g1f[:, at(((q + r) % 4) * 8, 8, 8), :].astype(BF16)
    g1_copies = to_slabs(lambda slab, r: g1x.at[r - 1], lambda r: g1r.at[r - 1], x1s, x1r)

    for p in range(OWN + 2):
        value = transposed(w1s, e1, p, 64)
        for i in range(16):
            igb[i, :, PLANE * p : PLANE * (p + 1)] = value[4 * i : 4 * i + 4].astype(BF16)
    ig_copies = []
    for r in (10, 8, 11, 9, 6, 14, 2, 7, 5, 15, 13, 4, 12, 3, 1):
        to = (m + r) % 16
        ig_copies.append(send(igb.at[to], igr.at[m], is_.at[r - 1], ir.at[r - 1], s, to))

    for c in gs_copies:
        c.wait_recv()
    mine16 = at(q * 16, 16, 16)
    for k in range(9):
        part = gsf[k, mine16, :]
        for r in range(3):
            part += gsr[r, k].astype(F32)
        part = part.astype(BF16)
        for dx in range(3):
            gp[3 * k + dx] = part[:, 128 * dx : 128 * dx + 128]

    gp_copies = []
    for r in range(1, 8):
        to = (s + r) % 8
        src = gp.at[pl.ds(4 * to, 4)]
        gp_copies.append(send(src, gpr.at[r - 1], ps.at[r - 1], pr.at[r - 1], to, m))

    for c in g1_copies:
        c.wait_recv()
    mine8 = at(q * 8, 8, 8)
    for k in range(9):
        part = g1f[k, mine8, :]
        for r in range(3):
            part += g1r[r, k].astype(F32)
        g1t[:, 192 * k : 192 * k + 192] = part
    g1b[...] = g1t[...].astype(BF16)
    total_copies = []
    for r in range(1, 8):
        to = (s + r) % 8
        total_copies.append(send(g1b, g1q.at[r - 1], g1s.at[r - 1], g1rr.at[r - 1], to, m))

    for c in feat_copies:
        c.wait_recv()
    fr[q] = fb[q]
    for i in range(4):
        feat[:, SLAB * i : SLAB * (i + 1)] = fr[i]
    for c in gp_copies:
        c.wait_recv()
    quarter = pl.ds(4 * s, 4)
    total = gp[quarter].astype(F32)
    for r in range(7):
        total += gpr[r].astype(F32)
    gq[quarter] = (total * scale).astype(BF16)
    gq_copies = []
    for r in range(1, 8):
        to = (s + r) % 8
        gq_copies.append(send(gq.at[quarter], gq.at[quarter], qs.at[r - 1], qr.at[r - 1], to, m))

    igr[m] = igb[m]
    for c in ig_copies:
        c.wait_recv()
    slabs = []
    for i in range(4):
        total = igr[i].astype(F32)
        for x in range(1, 4):
            total += igr[4 * x + i].astype(F32)
        slabs.append(total)
    for z in range(16):
        i, p = z // OWN, z % OWN
        total = slabs[i][:, PLANE * (p + 1) : PLANE * (p + 2)]
        if p == OWN - 1 and i < 3:
            total += slabs[i + 1][:, :PLANE]
        if p == 0 and i > 0:
            total += slabs[i - 1][:, PLANE * (OWN + 1) :]
        ig_out[:, PLANE * z : PLANE * (z + 1)] = total.astype(BF16)

    for c in total_copies:
        c.wait_recv()
    total = g1t[...]
    for r in range(7):
        total += g1q[r].astype(F32)
    g1_out[...] = total * scale

    for c in gq_copies:
        c.wait_recv()

    for c in waits:
        c.wait_send()


def finish(feat, ig, g1, gq, feat_out, ig_out, g1_out, g2_out):
    feat_out[...] = feat[...]
    ig_out[...] = ig[...]
    g1_out[...] = g1[...]
    for t in range(27):
        g2_out[:, 128 * t : 128 * t + 128] = gq[t].astype(F32)


def local_step(volumes, w_first, w_second, cotangent):
    cells = 4 * SLAB
    scale = 1.0 / math.sqrt(lax.axis_size("sample") * volumes.shape[1] * cells)
    V = pltpu.VMEM
    dma = pltpu.SemaphoreType.DMA
    scratch = [
        V((16, 4, WIDE2), BF16), V((4, 8, 1728), BF16), V((4, 16, 3456), BF16), V((4, 16, SLAB), BF16),
        V((288, 192), BF16), V((576, 384), BF16), V((64, 12 * PLANE), F32), V((192, WIDE2), BF16),
        V((288, WIDE2), F32), V((32, WIDE1), F32), V((128, WIDE1), BF16), V((384, WIDE1), BF16),
        V((576, WIDE1), F32), V((4, 16, SLAB), BF16), V((4, 16, SLAB), BF16), V((192, SLAB), BF16),
        V((128, WIDE1), BF16), V((6, 32, 2 * PLANE), BF16), V((8, 32, PLANE), BF16),
        V((96, SLAB), BF16), V((16, 4, WIDE1), BF16), V((16, 4, WIDE1), BF16),
        V((9, 64, 384), F32), V((3, 9, 16, 384), BF16), V((3, 9, 16, 384), BF16),
        V((32, 16, 128), BF16), V((7, 4, 16, 128), BF16),
        V((9, 32, 192), F32), V((3, 9, 8, 192), BF16), V((3, 9, 8, 192), BF16),
        V((8, 1728), F32), V((8, 1728), BF16), V((7, 8, 1728), BF16),
    ] + [
        dma((n,)) for n in
        (4, 15, 15, 3, 3, 3, 3, 3, 3, 6, 6, 3, 3, 6, 6, 8, 8, 3, 3, 15, 15, 3, 3, 7, 7, 7, 7, 7, 7)
    ]
    hbm = pl.BlockSpec(memory_space=pltpu.HBM)
    vmem = pl.BlockSpec(memory_space=pltpu.VMEM)
    parts = pl.pallas_call(
        functools.partial(kernel, scale),
        out_shape=(
            jax.ShapeDtypeStruct((16, cells), BF16),
            jax.ShapeDtypeStruct((4, cells), BF16),
            jax.ShapeDtypeStruct((8, 1728), F32),
            jax.ShapeDtypeStruct((32, 16, 128), BF16),
        ),
        in_specs=[hbm] * 4,
        out_specs=(vmem,) * 4,
        scratch_shapes=scratch,
        compiler_params=pltpu.CompilerParams(
            collective_id=0, has_side_effects=True, vmem_limit_bytes=48 * 1024 * 1024
        ),
    )(volumes.reshape(4, cells), w_first, w_second, cotangent.reshape(16, cells))
    feat, ig, g1, g2 = pl.pallas_call(
        finish,
        out_shape=(
            jax.ShapeDtypeStruct((16, cells), BF16),
            jax.ShapeDtypeStruct((4, cells), BF16),
            jax.ShapeDtypeStruct((8, 1728), F32),
            jax.ShapeDtypeStruct((16, 3456), F32),
        ),
        in_specs=[vmem] * 4,
        out_specs=(vmem,) * 4,
        compiler_params=pltpu.CompilerParams(vmem_limit_bytes=8 * 1024 * 1024),
    )(*parts)
    return feat.reshape(16, 1, cells), ig.reshape(4, 1, cells), g1, g2


def solution(mesh):
    return jax.shard_map(
        local_step,
        mesh=mesh,
        in_specs=(P("mp", "sample", None), P("mp", None), P("mp", None), P("mp", "sample", None)),
        out_specs=(P("mp", "sample", None), P("mp", "sample", None), P("mp", None), P("mp", None)),
        check_vma=False,
    )
```

```python
import functools
import math

import jax
import jax.numpy as jnp
from jax import lax
from jax.experimental import pallas as pl
from jax.experimental.pallas import tpu as pltpu
from jax.sharding import PartitionSpec as P

MESH = pl.DeviceIdType.MESH
F32 = jnp.float32
BF16 = jnp.bfloat16
PLANE = 256
OWN = 4
SLAB = OWN * PLANE
WIDE1 = SLAB + 2 * PLANE
WIDE2 = SLAB + 4 * PLANE


def at(start, size, unit):
    return pl.ds(pl.multiple_of(start, unit), size)


def plane_at(index, planes=1):
    return at(index * PLANE, planes * PLANE, PLANE)


def place(rows, lanes):
    return lax.broadcasted_iota(jnp.int32, (rows, lanes), 1)


def shifted_x(value, step):
    rows, lanes = value.shape
    x = place(rows, lanes) % 16
    if step > 0:
        return jnp.where(x < 15, pltpu.roll(value, lanes - 1, 1), 0.0)
    return jnp.where(x > 0, pltpu.roll(value, 1, 1), 0.0)


def shifted_y(value, step):
    rows, lanes = value.shape
    cell = place(rows, lanes)
    if step > 0:
        return jnp.where(cell < PLANE - 16, pltpu.roll(value, lanes - 16, 1), 0.0)
    return jnp.where(cell >= 16, pltpu.roll(value, 16, 1), 0.0)


def sigmoid(v):
    return 1.0 / (1.0 + jnp.exp(-v))


def slope(v):
    s = sigmoid(v)
    return s * (1.0 + v * (1.0 - s))


def mm(a, b, ca, cb):
    return lax.dot_general(a, b, (((ca,), (cb,)), ((), ())), preferred_element_type=F32)


def conv_plane(y_ref, rows, p):
    sums = []
    for dy in range(3):
        total = None
        for dz in range(3):
            k = 3 * dz + dy
            part = y_ref[rows * k : rows * (k + 1), plane_at(p + dz)]
            total = part if total is None else total + part
        sums.append(total)
    return sums[1] + shifted_y(sums[0], -1) + shifted_y(sums[2], 1)


def kernel(
    scale, vol, w1, w2, cot, feat, ig_out, g1_out, gq,
    vrecv, wb1, wb2, cb, w1s, w2s, vf, v3, y1, pre1, h, h3, y2, fb, fr, e2,
    ghb, ghr, ghe, e1, igb, igr, gsf, gsx, gsr, gp, gpr, g1f, g1x, g1r, g1t, g1b, g1q,
    loc, vs, vr, w1ss, w1sr, w2ss, w2sr, cs, cr, hs, hr, fs, frs, gs, gr, es, er, xs, xr,
    is_, ir, x1s, x1r, ps, pr, qs, qr, g1s, g1rr,
):
    s = lax.axis_index("sample")
    m = lax.axis_index("mp")
    col = m // 4
    q = m % 4
    waits = []

    def send(src, dst, ssem, rsem, sample, mp):
        c = pltpu.make_async_remote_copy(
            src_ref=src, dst_ref=dst, send_sem=ssem, recv_sem=rsem,
            device_id=(sample, mp), device_id_type=MESH,
        )
        c.start()
        waits.append(c)
        return c

    def slab_peer(r):
        return col * 4 + (q + r) % 4

    def col_peer(r):
        return ((col + r) % 4) * 4 + q

    def to_slabs(source, dst, ssem, rsem):
        return [
            send(source((q + r) % 4, r), dst(r), ssem.at[r - 1], rsem.at[r - 1], s, slab_peer(r))
            for r in (2, 1, 3)
        ]

    barrier = pltpu.get_barrier_semaphore()
    for r in range(1, 16):
        pl.semaphore_signal(barrier, inc=1, device_id=(s, (m + r) % 16), device_id_type=MESH)
    for r in range(1, 8):
        pl.semaphore_signal(barrier, inc=1, device_id=((s + r) % 8, m), device_id_type=MESH)

    def vol_part(slab):
        first = jnp.clip(slab * OWN - 2, 0, 8)
        return vol.at[:, plane_at(first, OWN + 4)]

    def slab_at(slab):
        return at(slab * SLAB, SLAB, SLAB)

    local = [
        pltpu.make_async_copy(vol_part(q), vrecv.at[m], loc.at[0]),
        pltpu.make_async_copy(w1, wb1.at[q], loc.at[1]),
        pltpu.make_async_copy(w2, wb2.at[q], loc.at[2]),
        pltpu.make_async_copy(cot.at[:, slab_at(q)], cb.at[q], loc.at[3]),
    ]
    for c in local:
        c.start()
    gp[27:32] = jnp.zeros((5, 16, 128), BF16)
    vf[...] = jnp.zeros(vf.shape, F32)
    pl.semaphore_wait(barrier, 22)

    vol_copies = []
    for r in (10, 8, 11, 9, 6, 14, 2, 7, 5, 15, 13, 4, 12, 3, 1):
        to = (m + r) % 16
        vol_copies.append(send(vol_part(to % 4), vrecv.at[m], vs.at[r - 1], vr.at[r - 1], s, to))
    w1_copies = to_slabs(lambda slab, r: w1, lambda r: wb1.at[q], w1ss, w1sr)

    local[1].wait()
    for c in w1_copies:
        c.wait_recv()
    w1_all = jnp.concatenate([wb1[i].astype(F32) for i in range(4)], axis=0)
    for k in range(9):
        w1s[32 * k : 32 * k + 32, :] = w1_all[:, 192 * k : 192 * k + 192].astype(BF16)
    local[0].wait()
    for c in vol_copies:
        c.wait_recv()
    core_peer = col * 4 + q + 1 - 2 * (q % 2)
    w2_core = send(w2, wb2.at[q], w2ss.at[0], w2sr.at[0], s, core_peer)
    w2_far = send(w2, wb2.at[q], w2ss.at[1], w2sr.at[1], s, slab_peer(2))
    cot_copies = to_slabs(lambda slab, r: cot.at[:, slab_at(slab)], lambda r: cb.at[q], cs, cr)
    first = jnp.clip(q * OWN - 2, 0, 8) - q * OWN + 4
    for i in range(16):
        vf[4 * i : 4 * i + 4, plane_at(first, OWN + 4)] = vrecv[i].astype(F32)

    for p in range(8):
        lanes = slice(PLANE * p, PLANE * (p + 1))
        value = vf[:, PLANE * (p + 2) : PLANE * (p + 3)]
        for dx in range(3):
            part = value if dx == 1 else shifted_x(value, dx - 1)
            v3[64 * dx : 64 * dx + 64, lanes] = part.astype(BF16)
        y1[:, lanes] = mm(w1s[...], v3[:, lanes], 1, 0)

    rows32 = at(col * 32, 32, 32)
    h_copies = []
    for half in range(2):
        for p in range(3 * half, 3 * half + 3):
            lanes = slice(PLANE * p, PLANE * (p + 1))
            value = conv_plane(y1, 32, p)
            pre1[:, lanes] = value
            z = q * OWN + p - 1
            inside = jnp.logical_and(z >= 0, z < 16)
            hidden = jnp.where(inside, value * sigmoid(value), 0.0)
            h[rows32, lanes] = hidden.astype(BF16)
        part = h.at[rows32, 3 * half * PLANE : 3 * (half + 1) * PLANE]
        for r in (2, 1, 3):
            i = 3 * half + r - 1
            h_copies.append(send(part, part, hs.at[i], hr.at[i], s, col_peer(r)))

    far = wb2.at[(q + 2) % 4]
    w2_far.wait_recv()
    w2_pass = send(far, far, w2ss.at[2], w2sr.at[2], s, core_peer)
    local[2].wait()
    w2_core.wait_recv()
    w2_pass.wait_recv()
    for k in range(9):
        for c in range(4):
            w2s[64 * k + 16 * c : 64 * k + 16 * c + 16, :] = wb2[c, :, 384 * k : 384 * k + 384]
    for half in range(2):
        for c in h_copies[3 * half : 3 * half + 3]:
            c.wait_recv()
        for p in range(3 * half, 3 * half + 3):
            lanes = slice(PLANE * p, PLANE * (p + 1))
            value = h[:, lanes].astype(F32)
            for dx in range(3):
                part = value if dx == 1 else shifted_x(value, dx - 1)
                h3[128 * dx : 128 * dx + 128, lanes] = part.astype(BF16)
            y2[:, lanes] = mm(w2s[...], h3[:, lanes], 1, 0)

    def spread(value, dst, rows, p):
        lanes = slice(PLANE * p, PLANE * (p + 1))
        value = value.astype(BF16).astype(F32)
        dst[0:rows, lanes] = shifted_y(value, 1).astype(BF16)
        dst[rows : 2 * rows, lanes] = value.astype(BF16)
        dst[2 * rows : 3 * rows, lanes] = shifted_y(value, -1).astype(BF16)

    def transposed(w, e, i, rows):
        taps = [dz for dz in range(3) if 0 <= i - dz < OWN]
        parts = [e[:, PLANE * (i - dz) : PLANE * (i - dz + 1)] for dz in taps]
        size = e.shape[0]
        z = mm(w[size * taps[0] : size * (taps[-1] + 1), :], jnp.concatenate(parts, axis=0), 0, 0)
        return z[rows : 2 * rows] + shifted_x(z[:rows], 1) + shifted_x(z[2 * rows :], -1)

    local[3].wait()
    for c in cot_copies:
        c.wait_recv()
    for p in range(OWN):
        lanes = slice(PLANE * p, PLANE * (p + 1))
        value = conv_plane(y2, 64, p)
        sg = sigmoid(value)
        out = (value * sg).astype(BF16)
        for i in range(4):
            fb[i, :, lanes] = out[16 * i : 16 * i + 16]
        cots = jnp.concatenate([cb[i, :, lanes] for i in range(4)], axis=0)
        spread(cots.astype(F32) * (sg * (1.0 + value * (1.0 - sg))), e2, 64, p)

    edge_copies = []
    for side, i in enumerate((0, OWN + 1)):
        lanes = slice(PLANE * i, PLANE * (i + 1))
        ghb[:, lanes] = transposed(w2s, e2, i, 128).astype(BF16)
        for r in (2, 1, 3, 0):
            to = (col + r) % 4
            n = 4 * side + r
            src = ghb.at[at(to * 32, 32, 32), lanes]
            there = to * 4 + (q + 3 - 2 * side) % 4
            edge_copies.append(send(src, ghe.at[n], es.at[n], er.at[n], s, there))
    gh_copies = []
    for half in range(2):
        for i in (1 + 2 * half, 2 + 2 * half):
            lanes = slice(PLANE * i, PLANE * (i + 1))
            ghb[:, lanes] = transposed(w2s, e2, i, 128).astype(BF16)
        lanes = slice(PLANE * (1 + 2 * half), PLANE * (3 + 2 * half))
        for r in (2, 1, 3):
            to = (col + r) % 4
            n = 3 * half + r - 1
            src = ghb.at[at(to * 32, 32, 32), lanes]
            gh_copies.append(send(src, ghr.at[n], gs.at[n], gr.at[n], s, col_peer(r)))

    for dz in range(3):
        part = mm(e2[...], h3[:, PLANE * dz : PLANE * dz + SLAB], 1, 1)
        for dy in range(3):
            gsf[3 * dz + dy] = part[64 * dy : 64 * dy + 64]
    core, pair = q % 2, q // 2
    for i in range(2):
        gsx[i] = gsf[:, at((2 * i + 1 - core) * 16, 16, 16), :].astype(BF16)
    core_copy = send(gsx.at[0:2], gsr.at[0:2], xs.at[0], xr.at[0], s, core_peer)
    core_copy.wait_recv()
    gsx[2] = (gsf[:, at((2 * (1 - pair) + core) * 16, 16, 16), :] + gsr[1 - pair].astype(F32)).astype(BF16)
    pair_copy = send(gsx.at[2], gsr.at[2], xs.at[1], xr.at[1], s, slab_peer(2))

    for c in gh_copies + edge_copies:
        c.wait_recv()
    for p in range(OWN):
        lanes = slice(PLANE * (p + 1), PLANE * (p + 2))
        total = ghb[rows32, lanes].astype(F32)
        part = slice(PLANE * (p % 2), PLANE * (p % 2 + 1))
        for r in range(3):
            total += ghr[3 * (p // 2) + r, :, part].astype(F32)
        for edge, side, inside in ((0, 1, q > 0), (OWN - 1, 0, q < 3)):
            if p == edge:
                more = ghe[4 * side].astype(F32)
                for r in range(1, 4):
                    more += ghe[4 * side + r].astype(F32)
                total += jnp.where(inside, more, 0.0)
        spread(total * slope(pre1[:, lanes]), e1, 32, p)

    for dz in range(3):
        part = mm(e1[...], v3[:, PLANE * (1 + dz) : PLANE * (1 + dz) + SLAB], 1, 1)
        for dy in range(3):
            g1f[3 * dz + dy] = part[32 * dy : 32 * dy + 32]
    for r in range(1, 4):
        g1x[r - 1] = g1f[:, at(((q + r) % 4) * 8, 8, 8), :].astype(BF16)
    g1_copies = to_slabs(lambda slab, r: g1x.at[r - 1], lambda r: g1r.at[r - 1], x1s, x1r)

    for p in range(OWN + 2):
        value = transposed(w1s, e1, p, 64)
        for i in range(16):
            igb[i, :, PLANE * p : PLANE * (p + 1)] = value[4 * i : 4 * i + 4].astype(BF16)
    ig_copies = []
    for r in (10, 8, 11, 9, 6, 14, 2, 7, 5, 15, 13, 4, 12, 3, 1):
        to = (m + r) % 16
        ig_copies.append(send(igb.at[to], igr.at[m], is_.at[r - 1], ir.at[r - 1], s, to))

    pair_copy.wait_recv()
    for k in range(9):
        part = gsf[k, at(q * 16, 16, 16), :] + gsr[pair, k].astype(F32) + gsr[2, k].astype(F32)
        part = part.astype(BF16)
        for dx in range(3):
            gp[3 * k + dx] = part[:, 128 * dx : 128 * dx + 128]
    gp_copies = []
    for r in range(1, 8):
        to = (s + r) % 8
        src = gp.at[pl.ds(4 * to, 4)]
        gp_copies.append(send(src, gpr.at[r - 1], ps.at[r - 1], pr.at[r - 1], to, m))

    for c in g1_copies:
        c.wait_recv()
    mine8 = at(q * 8, 8, 8)
    for k in range(9):
        part = g1f[k, mine8, :]
        for r in range(3):
            part += g1r[r, k].astype(F32)
        g1t[:, 192 * k : 192 * k + 192] = part
    g1b[...] = g1t[...].astype(BF16)
    total_copies = []
    for r in range(1, 8):
        to = (s + r) % 8
        total_copies.append(send(g1b, g1q.at[r - 1], g1s.at[r - 1], g1rr.at[r - 1], to, m))
    feat_copies = to_slabs(lambda slab, r: fb.at[slab], lambda r: fr.at[q], fs, frs)

    for c in gp_copies:
        c.wait_recv()
    quarter = pl.ds(4 * s, 4)
    total = gp[quarter].astype(F32)
    for r in range(7):
        total += gpr[r].astype(F32)
    gq[quarter] = (total * scale).astype(BF16)
    gq_copies = []
    for r in range(1, 8):
        to = (s + r) % 8
        gq_copies.append(send(gq.at[quarter], gq.at[quarter], qs.at[r - 1], qr.at[r - 1], to, m))

    for c in feat_copies:
        c.wait_recv()
    fr[q] = fb[q]
    for i in range(4):
        feat[:, SLAB * i : SLAB * (i + 1)] = fr[i]
    igr[m] = igb[m]
    for c in ig_copies:
        c.wait_recv()
    slabs = []
    for i in range(4):
        total = igr[i].astype(F32)
        for x in range(1, 4):
            total += igr[4 * x + i].astype(F32)
        slabs.append(total)
    for z in range(16):
        i, p = z // OWN, z % OWN
        total = slabs[i][:, PLANE * (p + 1) : PLANE * (p + 2)]
        if p == OWN - 1 and i < 3:
            total += slabs[i + 1][:, :PLANE]
        if p == 0 and i > 0:
            total += slabs[i - 1][:, PLANE * (OWN + 1) :]
        ig_out[:, PLANE * z : PLANE * (z + 1)] = total.astype(BF16)

    for c in total_copies:
        c.wait_recv()
    total = g1t[...]
    for r in range(7):
        total += g1q[r].astype(F32)
    g1_out[...] = total * scale

    for c in gq_copies:
        c.wait_recv()

    for c in waits:
        c.wait_send()


def finish(feat, ig, g1, gq, feat_out, ig_out, g1_out, g2_out):
    feat_out[...] = feat[...]
    ig_out[...] = ig[...]
    g1_out[...] = g1[...]
    for t in range(27):
        g2_out[:, 128 * t : 128 * t + 128] = gq[t].astype(F32)


def local_step(volumes, w_first, w_second, cotangent):
    cells = 4 * SLAB
    scale = 1.0 / math.sqrt(lax.axis_size("sample") * volumes.shape[1] * cells)
    V = pltpu.VMEM
    dma = pltpu.SemaphoreType.DMA
    scratch = [
        V((16, 4, WIDE2), BF16), V((4, 8, 1728), BF16), V((4, 16, 3456), BF16), V((4, 16, SLAB), BF16),
        V((288, 192), BF16), V((576, 384), BF16), V((64, 12 * PLANE), F32), V((192, WIDE2), BF16),
        V((288, WIDE2), F32), V((32, WIDE1), F32), V((128, WIDE1), BF16), V((384, WIDE1), BF16),
        V((576, WIDE1), F32), V((4, 16, SLAB), BF16), V((4, 16, SLAB), BF16), V((192, SLAB), BF16),
        V((128, WIDE1), BF16), V((6, 32, 2 * PLANE), BF16), V((8, 32, PLANE), BF16),
        V((96, SLAB), BF16), V((16, 4, WIDE1), BF16), V((16, 4, WIDE1), BF16),
        V((9, 64, 384), F32), V((3, 9, 16, 384), BF16), V((3, 9, 16, 384), BF16),
        V((32, 16, 128), BF16), V((7, 4, 16, 128), BF16),
        V((9, 32, 192), F32), V((3, 9, 8, 192), BF16), V((3, 9, 8, 192), BF16),
        V((8, 1728), F32), V((8, 1728), BF16), V((7, 8, 1728), BF16),
    ] + [
        dma((n,)) for n in
        (4, 15, 15, 3, 3, 3, 3, 3, 3, 6, 6, 3, 3, 6, 6, 8, 8, 3, 3, 15, 15, 3, 3, 7, 7, 7, 7, 7, 7)
    ]
    hbm = pl.BlockSpec(memory_space=pltpu.HBM)
    given = (volumes.reshape(4, cells), w_first, w_second, cotangent.reshape(16, cells))
    given = [pltpu.with_memory_space_constraint(a, pltpu.HBM) for a in given]
    vmem = pl.BlockSpec(memory_space=pltpu.VMEM)
    parts = pl.pallas_call(
        functools.partial(kernel, scale),
        out_shape=(
            jax.ShapeDtypeStruct((16, cells), BF16),
            jax.ShapeDtypeStruct((4, cells), BF16),
            jax.ShapeDtypeStruct((8, 1728), F32),
            jax.ShapeDtypeStruct((32, 16, 128), BF16),
        ),
        in_specs=[hbm] * 4,
        out_specs=(vmem,) * 4,
        scratch_shapes=scratch,
        compiler_params=pltpu.CompilerParams(
            collective_id=0, has_side_effects=True, vmem_limit_bytes=48 * 1024 * 1024
        ),
    )(*given)
    feat, ig, g1, g2 = pl.pallas_call(
        finish,
        out_shape=(
            jax.ShapeDtypeStruct((16, cells), BF16),
            jax.ShapeDtypeStruct((4, cells), BF16),
            jax.ShapeDtypeStruct((8, 1728), F32),
            jax.ShapeDtypeStruct((16, 3456), F32),
        ),
        in_specs=[vmem] * 4,
        out_specs=(vmem,) * 4,
        compiler_params=pltpu.CompilerParams(vmem_limit_bytes=8 * 1024 * 1024),
    )(*parts)
    return feat.reshape(16, 1, cells), ig.reshape(4, 1, cells), g1, g2


def solution(mesh):
    return jax.shard_map(
        local_step,
        mesh=mesh,
        in_specs=(P("mp", "sample", None), P("mp", None), P("mp", None), P("mp", "sample", None)),
        out_specs=(P("mp", "sample", None), P("mp", "sample", None), P("mp", None), P("mp", None)),
        check_vma=False,
    )
```

```python
import functools
import math

import jax
import jax.numpy as jnp
from jax import lax
from jax.experimental import pallas as pl
from jax.experimental.pallas import tpu as pltpu
from jax.sharding import PartitionSpec as P

MESH = pl.DeviceIdType.MESH
F32 = jnp.float32
BF16 = jnp.bfloat16
PLANE = 256
OWN = 4
SLAB = OWN * PLANE
CHUNK = 2
WIDE1 = SLAB + 2 * PLANE
WIDE2 = SLAB + 4 * PLANE


def at(start, size, unit):
    return pl.ds(pl.multiple_of(start, unit), size)


def plane_at(index, planes=1):
    return at(index * PLANE, planes * PLANE, PLANE)


def place(rows, lanes):
    return lax.broadcasted_iota(jnp.int32, (rows, lanes), 1)


def shifted_x(value, step):
    rows, lanes = value.shape
    x = place(rows, lanes) % 16
    if step > 0:
        return jnp.where(x < 15, pltpu.roll(value, lanes - 1, 1), 0.0)
    return jnp.where(x > 0, pltpu.roll(value, 1, 1), 0.0)


def shifted_y(value, step):
    rows, lanes = value.shape
    cell = place(rows, lanes)
    if step > 0:
        return jnp.where(cell < PLANE - 16, pltpu.roll(value, lanes - 16, 1), 0.0)
    return jnp.where(cell >= 16, pltpu.roll(value, 16, 1), 0.0)


def sigmoid(v):
    return 1.0 / (1.0 + jnp.exp(-v))


def slope(v):
    s = sigmoid(v)
    return s * (1.0 + v * (1.0 - s))


def mm(a, b, ca, cb):
    return lax.dot_general(a, b, (((ca,), (cb,)), ((), ())), preferred_element_type=F32)


def conv_plane(y_ref, rows, p):
    sums = []
    for dy in range(3):
        total = None
        for dz in range(3):
            k = 3 * dz + dy
            part = y_ref[rows * k : rows * (k + 1), plane_at(p + dz)]
            total = part if total is None else total + part
        sums.append(total)
    return sums[1] + shifted_y(sums[0], -1) + shifted_y(sums[2], 1)


def kernel(
    scale, vol, w1, w2, cot, feat, ig_out, g1_out, gq,
    vrecv, wb1, wb2, cb, w1s, w2s, vf, v3, y1, pre1, h, h3, y2, fb, fr, e2,
    ghb, ghr, ghe, e1, igb, igr, gsf, gsx, gsr, gp, gpr, g1f, g1x, g1r, g1t, g1b, g1q,
    loc, vs, vr, w1ss, w1sr, w2ss, w2sr, cs, cr, hs, hr, fs, frs, gs, gr, es, er, xs, xr,
    is_, ir, x1s, x1r, ps, pr, qs, qr, g1s, g1rr,
):
    s = lax.axis_index("sample")
    m = lax.axis_index("mp")
    col = m // 4
    q = m % 4
    waits = []

    def send(src, dst, ssem, rsem, sample, mp):
        c = pltpu.make_async_remote_copy(
            src_ref=src, dst_ref=dst, send_sem=ssem, recv_sem=rsem,
            device_id=(sample, mp), device_id_type=MESH,
        )
        c.start()
        waits.append(c)
        return c

    def slab_peer(r):
        return col * 4 + (q + r) % 4

    def col_peer(r):
        return ((col + r) % 4) * 4 + q

    def to_slabs(source, dst, ssem, rsem):
        return [
            send(source((q + r) % 4, r), dst(r), ssem.at[r - 1], rsem.at[r - 1], s, slab_peer(r))
            for r in (2, 1, 3)
        ]

    barrier = pltpu.get_barrier_semaphore()
    for r in range(1, 16):
        pl.semaphore_signal(barrier, inc=1, device_id=(s, (m + r) % 16), device_id_type=MESH)
    for r in range(1, 8):
        pl.semaphore_signal(barrier, inc=1, device_id=((s + r) % 8, m), device_id_type=MESH)
    for r in range(1, 8):
        there = ((s + r) % 8, col * 4 + (q + 2) % 4)
        pl.semaphore_signal(barrier, inc=1, device_id=there, device_id_type=MESH)
    for r in (1, 3):
        there = ((s + 4) % 8, col * 4 + (q + r) % 4)
        pl.semaphore_signal(barrier, inc=1, device_id=there, device_id_type=MESH)

    def vol_part(slab):
        first = jnp.clip(slab * OWN - 2, 0, 8)
        return vol.at[:, plane_at(first, OWN + 4)]

    def slab_at(slab):
        return at(slab * SLAB, SLAB, SLAB)

    local = [
        pltpu.make_async_copy(vol_part(q), vrecv.at[m], loc.at[0]),
        pltpu.make_async_copy(w1, wb1.at[q], loc.at[1]),
        pltpu.make_async_copy(w2, wb2.at[q], loc.at[2]),
        pltpu.make_async_copy(cot.at[:, slab_at(q)], cb.at[q], loc.at[3]),
    ]
    for c in local:
        c.start()
    gp[:, 27:32] = jnp.zeros((2, 5, 16, 128), BF16)
    vf[...] = jnp.zeros(vf.shape, F32)
    pl.semaphore_wait(barrier, 31)

    vol_copies = []
    for r in (10, 8, 11, 9, 6, 14, 2, 7, 5, 15, 13, 4, 12, 3, 1):
        to = (m + r) % 16
        vol_copies.append(send(vol_part(to % 4), vrecv.at[m], vs.at[r - 1], vr.at[r - 1], s, to))
    w1_copies = to_slabs(lambda slab, r: w1, lambda r: wb1.at[q], w1ss, w1sr)
    core_peer = col * 4 + q + 1 - 2 * (q % 2)
    w2_core = send(w2, wb2.at[q], w2ss.at[0], w2sr.at[0], s, core_peer)
    w2_far = send(w2, wb2.at[q], w2ss.at[1], w2sr.at[1], s, slab_peer(2))

    local[1].wait()
    for c in w1_copies:
        c.wait_recv()
    w1_all = jnp.concatenate([wb1[i].astype(F32) for i in range(4)], axis=0)
    for k in range(9):
        w1s[32 * k : 32 * k + 32, :] = w1_all[:, 192 * k : 192 * k + 192].astype(BF16)
    local[0].wait()
    for c in vol_copies:
        c.wait_recv()
    cot_copies = to_slabs(lambda slab, r: cot.at[:, slab_at(slab)], lambda r: cb.at[q], cs, cr)
    first = jnp.clip(q * OWN - 2, 0, 8) - q * OWN + 4
    for i in range(16):
        vf[4 * i : 4 * i + 4, plane_at(first, OWN + 4)] = vrecv[i].astype(F32)

    def products_v(p):
        lanes = slice(PLANE * p, PLANE * (p + 1))
        value = vf[:, PLANE * (p + 2) : PLANE * (p + 3)]
        for dx in range(3):
            part = value if dx == 1 else shifted_x(value, dx - 1)
            v3[64 * dx : 64 * dx + 64, lanes] = part.astype(BF16)
        y1[:, lanes] = mm(w1s[...], v3[:, lanes], 1, 0)

    rows32 = at(col * 32, 32, 32)
    h_copies = []
    products_v(0)
    products_v(1)
    for p in range(OWN + 2):
        products_v(p + 2)
        lanes = slice(PLANE * p, PLANE * (p + 1))
        value = conv_plane(y1, 32, p)
        pre1[:, lanes] = value
        z = q * OWN + p - 1
        inside = jnp.logical_and(z >= 0, z < 16)
        hidden = jnp.where(inside, value * sigmoid(value), 0.0)
        h[rows32, lanes] = hidden.astype(BF16)
        if p % CHUNK == CHUNK - 1:
            part = h.at[rows32, PLANE * (p + 1 - CHUNK) : PLANE * (p + 1)]
            for r in (2, 1, 3):
                i = 3 * (p // CHUNK) + r - 1
                h_copies.append(send(part, part, hs.at[i], hr.at[i], s, col_peer(r)))

    far = wb2.at[(q + 2) % 4]
    w2_far.wait_recv()
    w2_pass = send(far, far, w2ss.at[2], w2sr.at[2], s, core_peer)
    local[2].wait()
    w2_core.wait_recv()
    w2_pass.wait_recv()
    for k in range(9):
        for c in range(4):
            w2s[64 * k + 16 * c : 64 * k + 16 * c + 16, :] = wb2[c, :, 384 * k : 384 * k + 384]
    for p in range(OWN + 2):
        if p % CHUNK == 0:
            for c in h_copies[3 * (p // CHUNK) : 3 * (p // CHUNK) + 3]:
                c.wait_recv()
        lanes = slice(PLANE * p, PLANE * (p + 1))
        value = h[:, lanes].astype(F32)
        for dx in range(3):
            part = value if dx == 1 else shifted_x(value, dx - 1)
            h3[128 * dx : 128 * dx + 128, lanes] = part.astype(BF16)
        y2[:, lanes] = mm(w2s[...], h3[:, lanes], 1, 0)

    def spread(value, dst, rows, p):
        lanes = slice(PLANE * p, PLANE * (p + 1))
        value = value.astype(BF16).astype(F32)
        dst[0:rows, lanes] = shifted_y(value, 1).astype(BF16)
        dst[rows : 2 * rows, lanes] = value.astype(BF16)
        dst[2 * rows : 3 * rows, lanes] = shifted_y(value, -1).astype(BF16)

    def transposed(w, e, i, rows):
        taps = [dz for dz in range(3) if 0 <= i - dz < OWN]
        parts = [e[:, PLANE * (i - dz) : PLANE * (i - dz + 1)] for dz in taps]
        size = e.shape[0]
        z = mm(w[size * taps[0] : size * (taps[-1] + 1), :], jnp.concatenate(parts, axis=0), 0, 0)
        return z[rows : 2 * rows] + shifted_x(z[:rows], 1) + shifted_x(z[2 * rows :], -1)

    local[3].wait()
    for c in cot_copies:
        c.wait_recv()
    for p in range(OWN):
        lanes = slice(PLANE * p, PLANE * (p + 1))
        value = conv_plane(y2, 64, p)
        sg = sigmoid(value)
        out = (value * sg).astype(BF16)
        for i in range(4):
            fb[i, :, lanes] = out[16 * i : 16 * i + 16]
        cots = jnp.concatenate([cb[i, :, lanes] for i in range(4)], axis=0)
        spread(cots.astype(F32) * (sg * (1.0 + value * (1.0 - sg))), e2, 64, p)

    edge_copies = []
    for side, i in enumerate((0, OWN + 1)):
        lanes = slice(PLANE * i, PLANE * (i + 1))
        ghb[:, lanes] = transposed(w2s, e2, i, 128).astype(BF16)
        for r in (2, 1, 3, 0):
            to = (col + r) % 4
            n = 4 * side + r
            src = ghb.at[at(to * 32, 32, 32), lanes]
            there = to * 4 + (q + 3 - 2 * side) % 4
            edge_copies.append(send(src, ghe.at[n], es.at[n], er.at[n], s, there))
    gh_copies = []
    for half in range(2):
        for i in (1 + 2 * half, 2 + 2 * half):
            lanes = slice(PLANE * i, PLANE * (i + 1))
            ghb[:, lanes] = transposed(w2s, e2, i, 128).astype(BF16)
        lanes = slice(PLANE * (1 + 2 * half), PLANE * (3 + 2 * half))
        for r in (2, 1, 3):
            to = (col + r) % 4
            n = 3 * half + r - 1
            src = ghb.at[at(to * 32, 32, 32), lanes]
            gh_copies.append(send(src, ghr.at[n], gs.at[n], gr.at[n], s, col_peer(r)))

    for dz in range(3):
        part = mm(e2[...], h3[:, PLANE * dz : PLANE * dz + SLAB], 1, 1)
        for dy in range(3):
            gsf[3 * dz + dy] = part[64 * dy : 64 * dy + 64]
    core, pair = q % 2, q // 2
    for i in range(2):
        gsx[i] = gsf[:, at((2 * i + 1 - core) * 16, 16, 16), :].astype(BF16)
    core_copy = send(gsx.at[0:2], gsr.at[0:2], xs.at[0], xr.at[0], s, core_peer)
    core_copy.wait_recv()
    for i in range(2):
        mine = at((2 * i + core) * 16, 16, 16)
        for k in range(9):
            part = (gsf[k, mine, :] + gsr[i, k].astype(F32)).astype(BF16)
            for dx in range(3):
                gp[i, 3 * k + dx] = part[:, 128 * dx : 128 * dx + 128]
    gp_copies = []
    for r in (8, 7, 9, 6, 10, 5, 11, 4, 12, 3, 13, 2, 14, 1, 15):
        to = (s * 2 + pair + r) % 16
        src = gp.at[to % 2, pl.ds(4 * (to // 2), 4)]
        there = col * 4 + (to % 2) * 2 + core
        gp_copies.append(send(src, gpr.at[r - 1], ps.at[r - 1], pr.at[r - 1], to // 2, there))

    for c in gh_copies + edge_copies:
        c.wait_recv()
    for p in range(OWN):
        lanes = slice(PLANE * (p + 1), PLANE * (p + 2))
        total = ghb[rows32, lanes].astype(F32)
        part = slice(PLANE * (p % 2), PLANE * (p % 2 + 1))
        for r in range(3):
            total += ghr[3 * (p // 2) + r, :, part].astype(F32)
        for edge, side, inside in ((0, 1, q > 0), (OWN - 1, 0, q < 3)):
            if p == edge:
                more = ghe[4 * side].astype(F32)
                for r in range(1, 4):
                    more += ghe[4 * side + r].astype(F32)
                total += jnp.where(inside, more, 0.0)
        spread(total * slope(pre1[:, lanes]), e1, 32, p)

    for dz in range(3):
        part = mm(e1[...], v3[:, PLANE * (1 + dz) : PLANE * (1 + dz) + SLAB], 1, 1)
        for dy in range(3):
            g1f[3 * dz + dy] = part[32 * dy : 32 * dy + 32]
    for i in range(4):
        g1x[i] = g1f[:, 8 * i : 8 * i + 8, :].astype(BF16)
    g1_copies = []
    for r in (2, 6, 3, 5, 1, 7, 4):
        to = ((s // 4) * 4 + q + r) % 8
        there = (to // 4) * 4 + s % 4
        src = g1x.at[to % 4]
        g1_copies.append(send(src, g1r.at[r - 1], x1s.at[r - 1], x1r.at[r - 1], there, col * 4 + to % 4))

    for p in range(OWN + 2):
        value = transposed(w1s, e1, p, 64)
        for i in range(16):
            igb[i, :, PLANE * p : PLANE * (p + 1)] = value[4 * i : 4 * i + 4].astype(BF16)
    ig_copies = []
    for r in (10, 8, 11, 9, 6, 14, 2, 7, 5, 15, 13, 4, 12, 3, 1):
        to = (m + r) % 16
        ig_copies.append(send(igb.at[to], igr.at[m], is_.at[r - 1], ir.at[r - 1], s, to))

    for c in gp_copies:
        c.wait_recv()
    quarter = pl.ds(4 * s, 4)
    total = gp[pair, quarter].astype(F32)
    for r in range(15):
        total += gpr[r].astype(F32)
    gq[quarter] = (total * scale).astype(BF16)
    gq_copies = []
    for r in range(1, 8):
        to = (s + r) % 8
        gq_copies.append(send(gq.at[quarter], gq.at[quarter], qs.at[r - 1], qr.at[r - 1], to, m))

    for c in g1_copies:
        c.wait_recv()
    mine8 = at(q * 8, 8, 8)
    for k in range(9):
        part = g1f[k, mine8, :]
        for r in range(7):
            part += g1r[r, k].astype(F32)
        g1t[:, 192 * k : 192 * k + 192] = part
    g1b[...] = g1t[...].astype(BF16)
    total_copies = []
    for r in (2, 1, 3):
        to = (s // 4) * 4 + (s + r) % 4
        total_copies.append(send(g1b, g1q.at[r - 1], g1s.at[r - 1], g1rr.at[r - 1], to, m))
    feat_copies = to_slabs(lambda slab, r: fb.at[slab], lambda r: fr.at[q], fs, frs)

    for c in feat_copies:
        c.wait_recv()
    fr[q] = fb[q]
    for i in range(4):
        feat[:, SLAB * i : SLAB * (i + 1)] = fr[i]
    igr[m] = igb[m]
    for c in ig_copies:
        c.wait_recv()
    slabs = []
    for i in range(4):
        total = igr[i].astype(F32)
        for x in range(1, 4):
            total += igr[4 * x + i].astype(F32)
        slabs.append(total)
    for z in range(16):
        i, p = z // OWN, z % OWN
        total = slabs[i][:, PLANE * (p + 1) : PLANE * (p + 2)]
        if p == OWN - 1 and i < 3:
            total += slabs[i + 1][:, :PLANE]
        if p == 0 and i > 0:
            total += slabs[i - 1][:, PLANE * (OWN + 1) :]
        ig_out[:, PLANE * z : PLANE * (z + 1)] = total.astype(BF16)

    for c in total_copies:
        c.wait_recv()
    total = g1t[...]
    for r in range(3):
        total += g1q[r].astype(F32)
    g1_out[...] = total * scale

    for c in gq_copies:
        c.wait_recv()

    for c in waits:
        c.wait_send()


def finish(feat, ig, g1, gq, feat_out, ig_out, g1_out, g2_out):
    feat_out[...] = feat[...]
    ig_out[...] = ig[...]
    g1_out[...] = g1[...]
    for t in range(27):
        g2_out[:, 128 * t : 128 * t + 128] = gq[t].astype(F32)


def local_step(volumes, w_first, w_second, cotangent):
    cells = 4 * SLAB
    scale = 1.0 / math.sqrt(lax.axis_size("sample") * volumes.shape[1] * cells)
    V = pltpu.VMEM
    dma = pltpu.SemaphoreType.DMA
    scratch = [
        V((16, 4, WIDE2), BF16), V((4, 8, 1728), BF16), V((4, 16, 3456), BF16), V((4, 16, SLAB), BF16),
        V((288, 192), BF16), V((576, 384), BF16), V((64, 12 * PLANE), F32), V((192, WIDE2), BF16),
        V((288, WIDE2), F32), V((32, WIDE1), F32), V((128, WIDE1), BF16), V((384, WIDE1), BF16),
        V((576, WIDE1), F32), V((4, 16, SLAB), BF16), V((4, 16, SLAB), BF16), V((192, SLAB), BF16),
        V((128, WIDE1), BF16), V((6, 32, 2 * PLANE), BF16), V((8, 32, PLANE), BF16),
        V((96, SLAB), BF16), V((16, 4, WIDE1), BF16), V((16, 4, WIDE1), BF16),
        V((9, 64, 384), F32), V((2, 9, 16, 384), BF16), V((2, 9, 16, 384), BF16),
        V((2, 32, 16, 128), BF16), V((15, 4, 16, 128), BF16),
        V((9, 32, 192), F32), V((4, 9, 8, 192), BF16), V((7, 9, 8, 192), BF16),
        V((8, 1728), F32), V((8, 1728), BF16), V((3, 8, 1728), BF16),
    ] + [
        dma((n,)) for n in
        (4, 15, 15, 3, 3, 3, 3, 3, 3, 18, 18, 3, 3, 6, 6, 8, 8, 3, 3, 15, 15, 7, 7, 15, 15, 7, 7, 3, 3)
    ]
    hbm = pl.BlockSpec(memory_space=pltpu.HBM)
    given = (volumes.reshape(4, cells), w_first, w_second, cotangent.reshape(16, cells))
    given = [pltpu.with_memory_space_constraint(a, pltpu.HBM) for a in given]
    vmem = pl.BlockSpec(memory_space=pltpu.VMEM)
    parts = pl.pallas_call(
        functools.partial(kernel, scale),
        out_shape=(
            jax.ShapeDtypeStruct((16, cells), BF16),
            jax.ShapeDtypeStruct((4, cells), BF16),
            jax.ShapeDtypeStruct((8, 1728), F32),
            jax.ShapeDtypeStruct((32, 16, 128), BF16),
        ),
        in_specs=[hbm] * 4,
        out_specs=(vmem,) * 4,
        scratch_shapes=scratch,
        compiler_params=pltpu.CompilerParams(
            collective_id=0, has_side_effects=True, vmem_limit_bytes=48 * 1024 * 1024
        ),
    )(*given)
    feat, ig, g1, g2 = pl.pallas_call(
        finish,
        out_shape=(
            jax.ShapeDtypeStruct((16, cells), BF16),
            jax.ShapeDtypeStruct((4, cells), BF16),
            jax.ShapeDtypeStruct((8, 1728), F32),
            jax.ShapeDtypeStruct((16, 3456), F32),
        ),
        in_specs=[vmem] * 4,
        out_specs=(vmem,) * 4,
        compiler_params=pltpu.CompilerParams(vmem_limit_bytes=8 * 1024 * 1024),
    )(*parts)
    return feat.reshape(16, 1, cells), ig.reshape(4, 1, cells), g1, g2


def solution(mesh):
    return jax.shard_map(
        local_step,
        mesh=mesh,
        in_specs=(P("mp", "sample", None), P("mp", None), P("mp", None), P("mp", "sample", None)),
        out_specs=(P("mp", "sample", None), P("mp", "sample", None), P("mp", None), P("mp", None)),
        check_vma=False,
    )
```

```python
import functools
import math

import jax
import jax.numpy as jnp
from jax import lax
from jax.experimental import pallas as pl
from jax.experimental.pallas import tpu as pltpu
from jax.sharding import PartitionSpec as P

MESH = pl.DeviceIdType.MESH
F32 = jnp.float32
BF16 = jnp.bfloat16
PLANE = 256
OWN = 4
SLAB = OWN * PLANE
CHUNK = 1
WIDE1 = SLAB + 2 * PLANE
WIDE2 = SLAB + 4 * PLANE


def at(start, size, unit):
    return pl.ds(pl.multiple_of(start, unit), size)


def plane_at(index, planes=1):
    return at(index * PLANE, planes * PLANE, PLANE)


def place(rows, lanes):
    return lax.broadcasted_iota(jnp.int32, (rows, lanes), 1)


def shifted_x(value, step):
    rows, lanes = value.shape
    x = place(rows, lanes) % 16
    if step > 0:
        return jnp.where(x < 15, pltpu.roll(value, lanes - 1, 1), 0.0)
    return jnp.where(x > 0, pltpu.roll(value, 1, 1), 0.0)


def shifted_y(value, step):
    rows, lanes = value.shape
    cell = place(rows, lanes)
    if step > 0:
        return jnp.where(cell < PLANE - 16, pltpu.roll(value, lanes - 16, 1), 0.0)
    return jnp.where(cell >= 16, pltpu.roll(value, 16, 1), 0.0)


def sigmoid(v):
    return 1.0 / (1.0 + jnp.exp(-v))


def slope(v):
    s = sigmoid(v)
    return s * (1.0 + v * (1.0 - s))


def mm(a, b, ca, cb):
    return lax.dot_general(a, b, (((ca,), (cb,)), ((), ())), preferred_element_type=F32)


def conv_plane(y_ref, rows, p):
    sums = []
    for dy in range(3):
        total = None
        for dz in range(3):
            k = 3 * dz + dy
            part = y_ref[rows * k : rows * (k + 1), plane_at(p + dz)]
            total = part if total is None else total + part
        sums.append(total)
    return sums[1] + shifted_y(sums[0], -1) + shifted_y(sums[2], 1)


def kernel(
    scale, vol, w1, w2, cot, feat, ig_out, g1_out, gq,
    vrecv, wb1, wb2, cb, w1s, w2s, vf, v3, y1, pre1, h, h3, y2, fb, fr, e2,
    ghb, ghr, ghe, e1, igb, igr, gsf, gsx, gsr, gp, gpr, g1f, g1x, g1r, g1t, g1b, g1q,
    loc, vs, vr, w1ss, w1sr, w2ss, w2sr, cs, cr, hs, hr, fs, frs, gs, gr, es, er, xs, xr,
    is_, ir, x1s, x1r, ps, pr, qs, qr, g1s, g1rr,
):
    s = lax.axis_index("sample")
    m = lax.axis_index("mp")
    col = m // 4
    q = m % 4
    waits = []

    def send(src, dst, ssem, rsem, sample, mp):
        c = pltpu.make_async_remote_copy(
            src_ref=src, dst_ref=dst, send_sem=ssem, recv_sem=rsem,
            device_id=(sample, mp), device_id_type=MESH,
        )
        c.start()
        waits.append(c)
        return c

    def slab_peer(r):
        return col * 4 + (q + r) % 4

    def col_peer(r):
        return ((col + r) % 4) * 4 + q

    def to_slabs(source, dst, ssem, rsem):
        return [
            send(source((q + r) % 4, r), dst(r), ssem.at[r - 1], rsem.at[r - 1], s, slab_peer(r))
            for r in (2, 1, 3)
        ]

    barrier = pltpu.get_barrier_semaphore()
    for r in range(1, 16):
        pl.semaphore_signal(barrier, inc=1, device_id=(s, (m + r) % 16), device_id_type=MESH)
    for r in range(1, 8):
        pl.semaphore_signal(barrier, inc=1, device_id=((s + r) % 8, m), device_id_type=MESH)
    for r in range(1, 8):
        there = ((s + r) % 8, col * 4 + (q + 2) % 4)
        pl.semaphore_signal(barrier, inc=1, device_id=there, device_id_type=MESH)
    for r in (1, 3):
        there = ((s + 4) % 8, col * 4 + (q + r) % 4)
        pl.semaphore_signal(barrier, inc=1, device_id=there, device_id_type=MESH)

    def vol_part(slab):
        first = jnp.clip(slab * OWN - 2, 0, 8)
        return vol.at[:, plane_at(first, OWN + 4)]

    def slab_at(slab):
        return at(slab * SLAB, SLAB, SLAB)

    local = [
        pltpu.make_async_copy(vol_part(q), vrecv.at[m], loc.at[0]),
        pltpu.make_async_copy(w1, wb1.at[q], loc.at[1]),
        pltpu.make_async_copy(w2, wb2.at[q], loc.at[2]),
        pltpu.make_async_copy(cot.at[:, slab_at(q)], cb.at[q], loc.at[3]),
    ]
    for c in local:
        c.start()
    gp[:, 27:32] = jnp.zeros((2, 5, 16, 128), BF16)
    vf[...] = jnp.zeros(vf.shape, F32)
    pl.semaphore_wait(barrier, 31)

    w1_copies = to_slabs(lambda slab, r: w1, lambda r: wb1.at[q], w1ss, w1sr)
    vol_copies = []
    for r in (10, 8, 11, 9, 6, 14, 2, 7, 5, 15, 13, 4, 12, 3, 1):
        to = (m + r) % 16
        vol_copies.append(send(vol_part(to % 4), vrecv.at[m], vs.at[r - 1], vr.at[r - 1], s, to))
    core_peer = col * 4 + q + 1 - 2 * (q % 2)
    w2_core = send(w2, wb2.at[q], w2ss.at[0], w2sr.at[0], s, core_peer)
    w2_far = send(w2, wb2.at[q], w2ss.at[1], w2sr.at[1], s, slab_peer(2))

    local[1].wait()
    for c in w1_copies:
        c.wait_recv()
    w1_all = jnp.concatenate([wb1[i].astype(F32) for i in range(4)], axis=0)
    for k in range(9):
        w1s[32 * k : 32 * k + 32, :] = w1_all[:, 192 * k : 192 * k + 192].astype(BF16)
    local[0].wait()
    for c in vol_copies:
        c.wait_recv()
    cot_copies = to_slabs(lambda slab, r: cot.at[:, slab_at(slab)], lambda r: cb.at[q], cs, cr)
    first = jnp.clip(q * OWN - 2, 0, 8) - q * OWN + 4
    for i in range(16):
        vf[4 * i : 4 * i + 4, plane_at(first, OWN + 4)] = vrecv[i].astype(F32)

    def products_v(p):
        lanes = slice(PLANE * p, PLANE * (p + 1))
        value = vf[:, PLANE * (p + 2) : PLANE * (p + 3)]
        for dx in range(3):
            part = value if dx == 1 else shifted_x(value, dx - 1)
            v3[64 * dx : 64 * dx + 64, lanes] = part.astype(BF16)
        y1[:, lanes] = mm(w1s[...], v3[:, lanes], 1, 0)

    rows32 = at(col * 32, 32, 32)
    h_copies = []
    products_v(0)
    products_v(1)
    for p in range(OWN + 2):
        products_v(p + 2)
        lanes = slice(PLANE * p, PLANE * (p + 1))
        value = conv_plane(y1, 32, p)
        pre1[:, lanes] = value
        z = q * OWN + p - 1
        inside = jnp.logical_and(z >= 0, z < 16)
        hidden = jnp.where(inside, value * sigmoid(value), 0.0)
        h[rows32, lanes] = hidden.astype(BF16)
        if p % CHUNK == CHUNK - 1:
            part = h.at[rows32, PLANE * (p + 1 - CHUNK) : PLANE * (p + 1)]
            for r in (2, 1, 3):
                i = 3 * (p // CHUNK) + r - 1
                h_copies.append(send(part, part, hs.at[i], hr.at[i], s, col_peer(r)))

    far = wb2.at[(q + 2) % 4]
    w2_far.wait_recv()
    w2_pass = send(far, far, w2ss.at[2], w2sr.at[2], s, core_peer)
    local[2].wait()
    w2_core.wait_recv()
    w2_pass.wait_recv()
    for k in range(9):
        for c in range(4):
            w2s[64 * k + 16 * c : 64 * k + 16 * c + 16, :] = wb2[c, :, 384 * k : 384 * k + 384]
    for p in range(OWN + 2):
        if p % CHUNK == 0:
            for c in h_copies[3 * (p // CHUNK) : 3 * (p // CHUNK) + 3]:
                c.wait_recv()
        lanes = slice(PLANE * p, PLANE * (p + 1))
        value = h[:, lanes].astype(F32)
        for dx in range(3):
            part = value if dx == 1 else shifted_x(value, dx - 1)
            h3[128 * dx : 128 * dx + 128, lanes] = part.astype(BF16)
        y2[:, lanes] = mm(w2s[...], h3[:, lanes], 1, 0)

    def spread(value, dst, rows, p):
        lanes = slice(PLANE * p, PLANE * (p + 1))
        value = value.astype(BF16).astype(F32)
        dst[0:rows, lanes] = shifted_y(value, 1).astype(BF16)
        dst[rows : 2 * rows, lanes] = value.astype(BF16)
        dst[2 * rows : 3 * rows, lanes] = shifted_y(value, -1).astype(BF16)

    def transposed(w, e, i, rows):
        taps = [dz for dz in range(3) if 0 <= i - dz < OWN]
        parts = [e[:, PLANE * (i - dz) : PLANE * (i - dz + 1)] for dz in taps]
        size = e.shape[0]
        z = mm(w[size * taps[0] : size * (taps[-1] + 1), :], jnp.concatenate(parts, axis=0), 0, 0)
        return z[rows : 2 * rows] + shifted_x(z[:rows], 1) + shifted_x(z[2 * rows :], -1)

    local[3].wait()
    for c in cot_copies:
        c.wait_recv()
    for p in range(OWN):
        lanes = slice(PLANE * p, PLANE * (p + 1))
        value = conv_plane(y2, 64, p)
        sg = sigmoid(value)
        out = (value * sg).astype(BF16)
        for i in range(4):
            fb[i, :, lanes] = out[16 * i : 16 * i + 16]
        cots = jnp.concatenate([cb[i, :, lanes] for i in range(4)], axis=0)
        spread(cots.astype(F32) * (sg * (1.0 + value * (1.0 - sg))), e2, 64, p)

    edge_copies = []
    for side, i in enumerate((0, OWN + 1)):
        lanes = slice(PLANE * i, PLANE * (i + 1))
        ghb[:, lanes] = transposed(w2s, e2, i, 128).astype(BF16)
        for r in (2, 1, 3, 0):
            to = (col + r) % 4
            n = 4 * side + r
            src = ghb.at[at(to * 32, 32, 32), lanes]
            there = to * 4 + (q + 3 - 2 * side) % 4
            edge_copies.append(send(src, ghe.at[n], es.at[n], er.at[n], s, there))
    gh_copies = []
    for half in range(2):
        for i in (1 + 2 * half, 2 + 2 * half):
            lanes = slice(PLANE * i, PLANE * (i + 1))
            ghb[:, lanes] = transposed(w2s, e2, i, 128).astype(BF16)
        lanes = slice(PLANE * (1 + 2 * half), PLANE * (3 + 2 * half))
        for r in (2, 1, 3):
            to = (col + r) % 4
            n = 3 * half + r - 1
            src = ghb.at[at(to * 32, 32, 32), lanes]
            gh_copies.append(send(src, ghr.at[n], gs.at[n], gr.at[n], s, col_peer(r)))

    for dz in range(3):
        part = mm(e2[...], h3[:, PLANE * dz : PLANE * dz + SLAB], 1, 1)
        for dy in range(3):
            gsf[3 * dz + dy] = part[64 * dy : 64 * dy + 64]
    core, pair = q % 2, q // 2
    for i in range(2):
        gsx[i] = gsf[:, at((2 * i + 1 - core) * 16, 16, 16), :].astype(BF16)
    core_copy = send(gsx.at[0:2], gsr.at[0:2], xs.at[0], xr.at[0], s, core_peer)
    core_copy.wait_recv()
    for i in range(2):
        mine = at((2 * i + core) * 16, 16, 16)
        for k in range(9):
            part = (gsf[k, mine, :] + gsr[i, k].astype(F32)).astype(BF16)
            for dx in range(3):
                gp[i, 3 * k + dx] = part[:, 128 * dx : 128 * dx + 128]
    gp_copies = []
    for r in (8, 7, 9, 6, 10, 5, 11, 4, 12, 3, 13, 2, 14, 1, 15):
        to = (s * 2 + pair + r) % 16
        src = gp.at[to % 2, pl.ds(4 * (to // 2), 4)]
        there = col * 4 + (to % 2) * 2 + core
        gp_copies.append(send(src, gpr.at[r - 1], ps.at[r - 1], pr.at[r - 1], to // 2, there))

    for c in gh_copies + edge_copies:
        c.wait_recv()
    for p in range(OWN):
        lanes = slice(PLANE * (p + 1), PLANE * (p + 2))
        total = ghb[rows32, lanes].astype(F32)
        part = slice(PLANE * (p % 2), PLANE * (p % 2 + 1))
        for r in range(3):
            total += ghr[3 * (p // 2) + r, :, part].astype(F32)
        for edge, side, inside in ((0, 1, q > 0), (OWN - 1, 0, q < 3)):
            if p == edge:
                more = ghe[4 * side].astype(F32)
                for r in range(1, 4):
                    more += ghe[4 * side + r].astype(F32)
                total += jnp.where(inside, more, 0.0)
        spread(total * slope(pre1[:, lanes]), e1, 32, p)

    for dz in range(3):
        part = mm(e1[...], v3[:, PLANE * (1 + dz) : PLANE * (1 + dz) + SLAB], 1, 1)
        for dy in range(3):
            g1f[3 * dz + dy] = part[32 * dy : 32 * dy + 32]
    for i in range(4):
        g1x[i] = g1f[:, 8 * i : 8 * i + 8, :].astype(BF16)
    g1_copies = []
    for r in (2, 6, 3, 5, 1, 7, 4):
        to = ((s // 4) * 4 + q + r) % 8
        there = (to // 4) * 4 + s % 4
        src = g1x.at[to % 4]
        g1_copies.append(send(src, g1r.at[r - 1], x1s.at[r - 1], x1r.at[r - 1], there, col * 4 + to % 4))

    for p in range(OWN + 2):
        value = transposed(w1s, e1, p, 64)
        for i in range(16):
            igb[i, :, PLANE * p : PLANE * (p + 1)] = value[4 * i : 4 * i + 4].astype(BF16)
    ig_copies = []
    for r in (10, 8, 11, 9, 6, 14, 2, 7, 5, 15, 13, 4, 12, 3, 1):
        to = (m + r) % 16
        ig_copies.append(send(igb.at[to], igr.at[m], is_.at[r - 1], ir.at[r - 1], s, to))

    for c in gp_copies:
        c.wait_recv()
    quarter = pl.ds(4 * s, 4)
    total = gp[pair, quarter].astype(F32)
    for r in range(15):
        total += gpr[r].astype(F32)
    gq[quarter] = (total * scale).astype(BF16)
    gq_copies = []
    for r in range(1, 8):
        to = (s + r) % 8
        gq_copies.append(send(gq.at[quarter], gq.at[quarter], qs.at[r - 1], qr.at[r - 1], to, m))

    for c in g1_copies:
        c.wait_recv()
    mine8 = at(q * 8, 8, 8)
    for k in range(9):
        part = g1f[k, mine8, :]
        for r in range(7):
            part += g1r[r, k].astype(F32)
        g1t[:, 192 * k : 192 * k + 192] = part
    g1b[...] = g1t[...].astype(BF16)
    total_copies = []
    for r in (2, 1, 3):
        to = (s // 4) * 4 + (s + r) % 4
        total_copies.append(send(g1b, g1q.at[r - 1], g1s.at[r - 1], g1rr.at[r - 1], to, m))
    feat_copies = to_slabs(lambda slab, r: fb.at[slab], lambda r: fr.at[q], fs, frs)

    for c in feat_copies:
        c.wait_recv()
    fr[q] = fb[q]
    for i in range(4):
        feat[:, SLAB * i : SLAB * (i + 1)] = fr[i]
    igr[m] = igb[m]
    for c in ig_copies:
        c.wait_recv()
    slabs = []
    for i in range(4):
        total = igr[i].astype(F32)
        for x in range(1, 4):
            total += igr[4 * x + i].astype(F32)
        slabs.append(total)
    for z in range(16):
        i, p = z // OWN, z % OWN
        total = slabs[i][:, PLANE * (p + 1) : PLANE * (p + 2)]
        if p == OWN - 1 and i < 3:
            total += slabs[i + 1][:, :PLANE]
        if p == 0 and i > 0:
            total += slabs[i - 1][:, PLANE * (OWN + 1) :]
        ig_out[:, PLANE * z : PLANE * (z + 1)] = total.astype(BF16)

    for c in total_copies:
        c.wait_recv()
    total = g1t[...]
    for r in range(3):
        total += g1q[r].astype(F32)
    g1_out[...] = total * scale

    for c in gq_copies:
        c.wait_recv()

    for c in waits:
        c.wait_send()


def finish(feat, ig, g1, gq, feat_out, ig_out, g1_out, g2_out):
    feat_out[...] = feat[...]
    ig_out[...] = ig[...]
    g1_out[...] = g1[...]
    for t in range(27):
        g2_out[:, 128 * t : 128 * t + 128] = gq[t].astype(F32)


def local_step(volumes, w_first, w_second, cotangent):
    cells = 4 * SLAB
    scale = 1.0 / math.sqrt(lax.axis_size("sample") * volumes.shape[1] * cells)
    V = pltpu.VMEM
    dma = pltpu.SemaphoreType.DMA
    scratch = [
        V((16, 4, WIDE2), BF16), V((4, 8, 1728), BF16), V((4, 16, 3456), BF16), V((4, 16, SLAB), BF16),
        V((288, 192), BF16), V((576, 384), BF16), V((64, 12 * PLANE), F32), V((192, WIDE2), BF16),
        V((288, WIDE2), F32), V((32, WIDE1), F32), V((128, WIDE1), BF16), V((384, WIDE1), BF16),
        V((576, WIDE1), F32), V((4, 16, SLAB), BF16), V((4, 16, SLAB), BF16), V((192, SLAB), BF16),
        V((128, WIDE1), BF16), V((6, 32, 2 * PLANE), BF16), V((8, 32, PLANE), BF16),
        V((96, SLAB), BF16), V((16, 4, WIDE1), BF16), V((16, 4, WIDE1), BF16),
        V((9, 64, 384), F32), V((2, 9, 16, 384), BF16), V((2, 9, 16, 384), BF16),
        V((2, 32, 16, 128), BF16), V((15, 4, 16, 128), BF16),
        V((9, 32, 192), F32), V((4, 9, 8, 192), BF16), V((7, 9, 8, 192), BF16),
        V((8, 1728), F32), V((8, 1728), BF16), V((3, 8, 1728), BF16),
    ] + [
        dma((n,)) for n in
        (4, 15, 15, 3, 3, 3, 3, 3, 3, 18, 18, 3, 3, 6, 6, 8, 8, 3, 3, 15, 15, 7, 7, 15, 15, 7, 7, 3, 3)
    ]
    hbm = pl.BlockSpec(memory_space=pltpu.HBM)
    given = (volumes.reshape(4, cells), w_first, w_second, cotangent.reshape(16, cells))
    given = [pltpu.with_memory_space_constraint(a, pltpu.HBM) for a in given]
    vmem = pl.BlockSpec(memory_space=pltpu.VMEM)
    parts = pl.pallas_call(
        functools.partial(kernel, scale),
        out_shape=(
            jax.ShapeDtypeStruct((16, cells), BF16),
            jax.ShapeDtypeStruct((4, cells), BF16),
            jax.ShapeDtypeStruct((8, 1728), F32),
            jax.ShapeDtypeStruct((32, 16, 128), BF16),
        ),
        in_specs=[hbm] * 4,
        out_specs=(vmem,) * 4,
        scratch_shapes=scratch,
        compiler_params=pltpu.CompilerParams(
            collective_id=0, has_side_effects=True, vmem_limit_bytes=48 * 1024 * 1024
        ),
    )(*given)
    feat, ig, g1, g2 = pl.pallas_call(
        finish,
        out_shape=(
            jax.ShapeDtypeStruct((16, cells), BF16),
            jax.ShapeDtypeStruct((4, cells), BF16),
            jax.ShapeDtypeStruct((8, 1728), F32),
            jax.ShapeDtypeStruct((16, 3456), F32),
        ),
        in_specs=[vmem] * 4,
        out_specs=(vmem,) * 4,
        compiler_params=pltpu.CompilerParams(vmem_limit_bytes=8 * 1024 * 1024),
    )(*parts)
    return feat.reshape(16, 1, cells), ig.reshape(4, 1, cells), g1, g2


def solution(mesh):
    return jax.shard_map(
        local_step,
        mesh=mesh,
        in_specs=(P("mp", "sample", None), P("mp", None), P("mp", None), P("mp", "sample", None)),
        out_specs=(P("mp", "sample", None), P("mp", "sample", None), P("mp", None), P("mp", None)),
        check_vma=False,
    )
```

```python
import functools
import math

import jax
import jax.numpy as jnp
from jax import lax
from jax.experimental import pallas as pl
from jax.experimental.pallas import tpu as pltpu
from jax.sharding import PartitionSpec as P

MESH = pl.DeviceIdType.MESH
F32 = jnp.float32
BF16 = jnp.bfloat16
PLANE = 256
OWN = 4
SLAB = OWN * PLANE
CHUNK = 1
WIDE1 = SLAB + 2 * PLANE
WIDE2 = SLAB + 4 * PLANE


def at(start, size, unit):
    return pl.ds(pl.multiple_of(start, unit), size)


def plane_at(index, planes=1):
    return at(index * PLANE, planes * PLANE, PLANE)


def place(rows, lanes):
    return lax.broadcasted_iota(jnp.int32, (rows, lanes), 1)


def shifted_x(value, step):
    rows, lanes = value.shape
    x = place(rows, lanes) % 16
    if step > 0:
        return jnp.where(x < 15, pltpu.roll(value, lanes - 1, 1), 0.0)
    return jnp.where(x > 0, pltpu.roll(value, 1, 1), 0.0)


def shifted_y(value, step):
    rows, lanes = value.shape
    cell = place(rows, lanes)
    if step > 0:
        return jnp.where(cell < PLANE - 16, pltpu.roll(value, lanes - 16, 1), 0.0)
    return jnp.where(cell >= 16, pltpu.roll(value, 16, 1), 0.0)


def sigmoid(v):
    return 1.0 / (1.0 + jnp.exp(-v))


def slope(v):
    s = sigmoid(v)
    return s * (1.0 + v * (1.0 - s))


def mm(a, b, ca, cb):
    return lax.dot_general(a, b, (((ca,), (cb,)), ((), ())), preferred_element_type=F32)


def conv_plane(y_ref, rows, p):
    sums = []
    for dy in range(3):
        total = None
        for dz in range(3):
            k = 3 * dz + dy
            part = y_ref[rows * k : rows * (k + 1), plane_at(p + dz)]
            total = part if total is None else total + part
        sums.append(total)
    return sums[1] + shifted_y(sums[0], -1) + shifted_y(sums[2], 1)


def kernel(
    scale, vol, w1, w2, cot, feat, ig_out, g1_out, gq,
    vrecv, wb1, wb2, cb, w1s, w2s, vf, v3, y1, pre1, h, h3, y2, fb, fr, e2,
    ghb, ghr, ghe, e1, igb, igr, gsf, gsx, gsr, gp, gpr, g1f, g1x, g1r, g1t, g1b, g1q,
    loc, vs, vr, w1ss, w1sr, w2ss, w2sr, cs, cr, hs, hr, fs, frs, gs, gr, es, er, xs, xr,
    is_, ir, x1s, x1r, ps, pr, qs, qr, g1s, g1rr,
):
    s = lax.axis_index("sample")
    m = lax.axis_index("mp")
    col = m // 4
    q = m % 4
    waits = []

    def send(src, dst, ssem, rsem, sample, mp):
        c = pltpu.make_async_remote_copy(
            src_ref=src, dst_ref=dst, send_sem=ssem, recv_sem=rsem,
            device_id=(sample, mp), device_id_type=MESH,
        )
        c.start()
        waits.append(c)
        return c

    def slab_peer(r):
        return col * 4 + (q + r) % 4

    def col_peer(r):
        return ((col + r) % 4) * 4 + q

    def to_slabs(source, dst, ssem, rsem):
        return [
            send(source((q + r) % 4, r), dst(r), ssem.at[r - 1], rsem.at[r - 1], s, slab_peer(r))
            for r in (2, 1, 3)
        ]

    barrier = pltpu.get_barrier_semaphore()
    for r in range(1, 16):
        pl.semaphore_signal(barrier, inc=1, device_id=(s, (m + r) % 16), device_id_type=MESH)
    for r in range(1, 8):
        pl.semaphore_signal(barrier, inc=1, device_id=((s + r) % 8, m), device_id_type=MESH)
    for r in range(1, 8):
        there = ((s + r) % 8, col * 4 + (q + 2) % 4)
        pl.semaphore_signal(barrier, inc=1, device_id=there, device_id_type=MESH)
    for r in (1, 3):
        there = ((s + 4) % 8, col * 4 + (q + r) % 4)
        pl.semaphore_signal(barrier, inc=1, device_id=there, device_id_type=MESH)

    def vol_part(slab):
        first = jnp.clip(slab * OWN - 2, 0, 8)
        return vol.at[:, plane_at(first, OWN + 4)]

    def slab_at(slab):
        return at(slab * SLAB, SLAB, SLAB)

    local = [
        pltpu.make_async_copy(vol_part(q), vrecv.at[m], loc.at[0]),
        pltpu.make_async_copy(w1, wb1.at[q], loc.at[1]),
        pltpu.make_async_copy(w2, wb2.at[q], loc.at[2]),
        pltpu.make_async_copy(cot.at[:, slab_at(q)], cb.at[q], loc.at[3]),
    ]
    for c in local:
        c.start()
    gp[:, 27:32] = jnp.zeros((2, 5, 16, 128), BF16)
    vf[...] = jnp.zeros(vf.shape, F32)
    pl.semaphore_wait(barrier, 31)

    w1_copies = to_slabs(lambda slab, r: w1, lambda r: wb1.at[q], w1ss, w1sr)
    vol_copies = []
    for r in (10, 8, 11, 9, 6, 14, 2, 7, 5, 15, 13, 4, 12, 3, 1):
        to = (m + r) % 16
        vol_copies.append(send(vol_part(to % 4), vrecv.at[m], vs.at[r - 1], vr.at[r - 1], s, to))
    core_peer = col * 4 + q + 1 - 2 * (q % 2)
    w2_core = send(w2, wb2.at[q], w2ss.at[0], w2sr.at[0], s, core_peer)
    w2_far = send(w2, wb2.at[q], w2ss.at[1], w2sr.at[1], s, slab_peer(2))

    local[1].wait()
    for c in w1_copies:
        c.wait_recv()
    w1_all = jnp.concatenate([wb1[i].astype(F32) for i in range(4)], axis=0)
    for k in range(9):
        w1s[32 * k : 32 * k + 32, :] = w1_all[:, 192 * k : 192 * k + 192].astype(BF16)
    local[0].wait()
    for c in vol_copies:
        c.wait_recv()
    cot_copies = to_slabs(lambda slab, r: cot.at[:, slab_at(slab)], lambda r: cb.at[q], cs, cr)
    first = jnp.clip(q * OWN - 2, 0, 8) - q * OWN + 4
    for i in range(16):
        vf[4 * i : 4 * i + 4, plane_at(first, OWN + 4)] = vrecv[i].astype(F32)

    def products_v(p):
        lanes = slice(PLANE * p, PLANE * (p + 1))
        value = vf[:, PLANE * (p + 2) : PLANE * (p + 3)]
        for dx in range(3):
            part = value if dx == 1 else shifted_x(value, dx - 1)
            v3[64 * dx : 64 * dx + 64, lanes] = part.astype(BF16)
        y1[:, lanes] = mm(w1s[...], v3[:, lanes], 1, 0)

    rows32 = at(col * 32, 32, 32)
    h_copies = []
    products_v(0)
    products_v(1)
    for p in range(OWN + 2):
        products_v(p + 2)
        lanes = slice(PLANE * p, PLANE * (p + 1))
        value = conv_plane(y1, 32, p)
        pre1[:, lanes] = value
        z = q * OWN + p - 1
        inside = jnp.logical_and(z >= 0, z < 16)
        hidden = jnp.where(inside, value * sigmoid(value), 0.0)
        h[rows32, lanes] = hidden.astype(BF16)
        if p % CHUNK == CHUNK - 1:
            part = h.at[rows32, PLANE * (p + 1 - CHUNK) : PLANE * (p + 1)]
            for r in (2, 1, 3):
                i = 3 * (p // CHUNK) + r - 1
                h_copies.append(send(part, part, hs.at[i], hr.at[i], s, col_peer(r)))

    far = wb2.at[(q + 2) % 4]
    w2_far.wait_recv()
    w2_pass = send(far, far, w2ss.at[2], w2sr.at[2], s, core_peer)
    local[2].wait()
    w2_core.wait_recv()
    w2_pass.wait_recv()
    for k in range(9):
        for c in range(4):
            w2s[64 * k + 16 * c : 64 * k + 16 * c + 16, :] = wb2[c, :, 384 * k : 384 * k + 384]
    for p in range(OWN + 2):
        if p % CHUNK == 0:
            for c in h_copies[3 * (p // CHUNK) : 3 * (p // CHUNK) + 3]:
                c.wait_recv()
        lanes = slice(PLANE * p, PLANE * (p + 1))
        value = h[:, lanes].astype(F32)
        for dx in range(3):
            part = value if dx == 1 else shifted_x(value, dx - 1)
            h3[128 * dx : 128 * dx + 128, lanes] = part.astype(BF16)
        y2[:, lanes] = mm(w2s[...], h3[:, lanes], 1, 0)

    def spread(value, dst, rows, p):
        lanes = slice(PLANE * p, PLANE * (p + 1))
        value = value.astype(BF16).astype(F32)
        dst[0:rows, lanes] = shifted_y(value, 1).astype(BF16)
        dst[rows : 2 * rows, lanes] = value.astype(BF16)
        dst[2 * rows : 3 * rows, lanes] = shifted_y(value, -1).astype(BF16)

    def transposed(w, e, i, rows):
        taps = [dz for dz in range(3) if 0 <= i - dz < OWN]
        parts = [e[:, PLANE * (i - dz) : PLANE * (i - dz + 1)] for dz in taps]
        size = e.shape[0]
        z = mm(w[size * taps[0] : size * (taps[-1] + 1), :], jnp.concatenate(parts, axis=0), 0, 0)
        return z[rows : 2 * rows] + shifted_x(z[:rows], 1) + shifted_x(z[2 * rows :], -1)

    local[3].wait()
    for c in cot_copies:
        c.wait_recv()
    for p in range(OWN):
        lanes = slice(PLANE * p, PLANE * (p + 1))
        value = conv_plane(y2, 64, p)
        sg = sigmoid(value)
        out = (value * sg).astype(BF16)
        for i in range(4):
            fb[i, :, lanes] = out[16 * i : 16 * i + 16]
        cots = jnp.concatenate([cb[i, :, lanes] for i in range(4)], axis=0)
        spread(cots.astype(F32) * (sg * (1.0 + value * (1.0 - sg))), e2, 64, p)

    edge_copies = []
    for side, i in enumerate((0, OWN + 1)):
        lanes = slice(PLANE * i, PLANE * (i + 1))
        ghb[:, lanes] = transposed(w2s, e2, i, 128).astype(BF16)
        for r in (2, 1, 3, 0):
            to = (col + r) % 4
            n = 4 * side + r
            src = ghb.at[at(to * 32, 32, 32), lanes]
            there = to * 4 + (q + 3 - 2 * side) % 4
            edge_copies.append(send(src, ghe.at[n], es.at[n], er.at[n], s, there))
    gh_copies = []
    for i in range(1, OWN + 1):
        lanes = slice(PLANE * i, PLANE * (i + 1))
        ghb[:, lanes] = transposed(w2s, e2, i, 128).astype(BF16)
        for r in (2, 1, 3):
            to = (col + r) % 4
            n = 3 * (i - 1) + r - 1
            src = ghb.at[at(to * 32, 32, 32), lanes]
            gh_copies.append(send(src, ghr.at[n], gs.at[n], gr.at[n], s, col_peer(r)))

    for dz in range(3):
        part = mm(e2[...], h3[:, PLANE * dz : PLANE * dz + SLAB], 1, 1)
        for dy in range(3):
            gsf[3 * dz + dy] = part[64 * dy : 64 * dy + 64]
    core, pair = q % 2, q // 2
    for i in range(2):
        gsx[i] = gsf[:, at((2 * i + 1 - core) * 16, 16, 16), :].astype(BF16)
    core_copy = send(gsx.at[0:2], gsr.at[0:2], xs.at[0], xr.at[0], s, core_peer)
    core_copy.wait_recv()
    for i in range(2):
        mine = at((2 * i + core) * 16, 16, 16)
        for k in range(9):
            part = (gsf[k, mine, :] + gsr[i, k].astype(F32)).astype(BF16)
            for dx in range(3):
                gp[i, 3 * k + dx] = part[:, 128 * dx : 128 * dx + 128]
    gp_copies = []
    for r in (8, 7, 9, 6, 10, 5, 11, 4, 12, 3, 13, 2, 14, 1, 15):
        to = (s * 2 + pair + r) % 16
        src = gp.at[to % 2, pl.ds(4 * (to // 2), 4)]
        there = col * 4 + (to % 2) * 2 + core
        gp_copies.append(send(src, gpr.at[r - 1], ps.at[r - 1], pr.at[r - 1], to // 2, there))

    for p in (1, 2, 0, 3):
        for c in gh_copies[3 * p : 3 * p + 3]:
            c.wait_recv()
        for c in {0: edge_copies[4:], OWN - 1: edge_copies[:4]}.get(p, []):
            c.wait_recv()
        lanes = slice(PLANE * (p + 1), PLANE * (p + 2))
        total = ghb[rows32, lanes].astype(F32)
        for r in range(3):
            total += ghr[3 * p + r].astype(F32)
        for edge, side, inside in ((0, 1, q > 0), (OWN - 1, 0, q < 3)):
            if p == edge:
                more = ghe[4 * side].astype(F32)
                for r in range(1, 4):
                    more += ghe[4 * side + r].astype(F32)
                total += jnp.where(inside, more, 0.0)
        spread(total * slope(pre1[:, lanes]), e1, 32, p)

    for dz in range(3):
        part = mm(e1[...], v3[:, PLANE * (1 + dz) : PLANE * (1 + dz) + SLAB], 1, 1)
        for dy in range(3):
            g1f[3 * dz + dy] = part[32 * dy : 32 * dy + 32]
    for i in range(4):
        g1x[i] = g1f[:, 8 * i : 8 * i + 8, :].astype(BF16)
    g1_copies = []
    for r in (2, 6, 3, 5, 1, 7, 4):
        to = ((s // 4) * 4 + q + r) % 8
        there = (to // 4) * 4 + s % 4
        src = g1x.at[to % 4]
        g1_copies.append(send(src, g1r.at[r - 1], x1s.at[r - 1], x1r.at[r - 1], there, col * 4 + to % 4))

    for p in range(OWN + 2):
        value = transposed(w1s, e1, p, 64)
        for i in range(16):
            igb[i, :, PLANE * p : PLANE * (p + 1)] = value[4 * i : 4 * i + 4].astype(BF16)
    ig_copies = []
    for r in (10, 8, 11, 9, 6, 14, 2, 7, 5, 15, 13, 4, 12, 3, 1):
        to = (m + r) % 16
        ig_copies.append(send(igb.at[to], igr.at[m], is_.at[r - 1], ir.at[r - 1], s, to))

    for c in gp_copies:
        c.wait_recv()
    quarter = pl.ds(4 * s, 4)
    total = gp[pair, quarter].astype(F32)
    for r in range(15):
        total += gpr[r].astype(F32)
    gq[quarter] = (total * scale).astype(BF16)
    gq_copies = []
    for r in range(1, 8):
        to = (s + r) % 8
        gq_copies.append(send(gq.at[quarter], gq.at[quarter], qs.at[r - 1], qr.at[r - 1], to, m))

    for c in g1_copies:
        c.wait_recv()
    mine8 = at(q * 8, 8, 8)
    for k in range(9):
        part = g1f[k, mine8, :]
        for r in range(7):
            part += g1r[r, k].astype(F32)
        g1t[:, 192 * k : 192 * k + 192] = part
    g1b[...] = g1t[...].astype(BF16)
    total_copies = []
    for r in (2, 1, 3):
        to = (s // 4) * 4 + (s + r) % 4
        total_copies.append(send(g1b, g1q.at[r - 1], g1s.at[r - 1], g1rr.at[r - 1], to, m))
    feat_copies = to_slabs(lambda slab, r: fb.at[slab], lambda r: fr.at[q], fs, frs)

    for c in feat_copies:
        c.wait_recv()
    fr[q] = fb[q]
    for i in range(4):
        feat[:, SLAB * i : SLAB * (i + 1)] = fr[i]
    igr[m] = igb[m]
    for c in ig_copies:
        c.wait_recv()
    slabs = []
    for i in range(4):
        total = igr[i].astype(F32)
        for x in range(1, 4):
            total += igr[4 * x + i].astype(F32)
        slabs.append(total)
    for z in range(16):
        i, p = z // OWN, z % OWN
        total = slabs[i][:, PLANE * (p + 1) : PLANE * (p + 2)]
        if p == OWN - 1 and i < 3:
            total += slabs[i + 1][:, :PLANE]
        if p == 0 and i > 0:
            total += slabs[i - 1][:, PLANE * (OWN + 1) :]
        ig_out[:, PLANE * z : PLANE * (z + 1)] = total.astype(BF16)

    for c in total_copies:
        c.wait_recv()
    total = g1t[...]
    for r in range(3):
        total += g1q[r].astype(F32)
    g1_out[...] = total * scale

    for c in gq_copies:
        c.wait_recv()

    for c in waits:
        c.wait_send()


def finish(feat, ig, g1, gq, feat_out, ig_out, g1_out, g2_out):
    feat_out[...] = feat[...]
    ig_out[...] = ig[...]
    g1_out[...] = g1[...]
    for t in range(27):
        g2_out[:, 128 * t : 128 * t + 128] = gq[t].astype(F32)


def local_step(volumes, w_first, w_second, cotangent):
    cells = 4 * SLAB
    scale = 1.0 / math.sqrt(lax.axis_size("sample") * volumes.shape[1] * cells)
    V = pltpu.VMEM
    dma = pltpu.SemaphoreType.DMA
    scratch = [
        V((16, 4, WIDE2), BF16), V((4, 8, 1728), BF16), V((4, 16, 3456), BF16), V((4, 16, SLAB), BF16),
        V((288, 192), BF16), V((576, 384), BF16), V((64, 12 * PLANE), F32), V((192, WIDE2), BF16),
        V((288, WIDE2), F32), V((32, WIDE1), F32), V((128, WIDE1), BF16), V((384, WIDE1), BF16),
        V((576, WIDE1), F32), V((4, 16, SLAB), BF16), V((4, 16, SLAB), BF16), V((192, SLAB), BF16),
        V((128, WIDE1), BF16), V((12, 32, PLANE), BF16), V((8, 32, PLANE), BF16),
        V((96, SLAB), BF16), V((16, 4, WIDE1), BF16), V((16, 4, WIDE1), BF16),
        V((9, 64, 384), F32), V((2, 9, 16, 384), BF16), V((2, 9, 16, 384), BF16),
        V((2, 32, 16, 128), BF16), V((15, 4, 16, 128), BF16),
        V((9, 32, 192), F32), V((4, 9, 8, 192), BF16), V((7, 9, 8, 192), BF16),
        V((8, 1728), F32), V((8, 1728), BF16), V((3, 8, 1728), BF16),
    ] + [
        dma((n,)) for n in
        (4, 15, 15, 3, 3, 3, 3, 3, 3, 18, 18, 3, 3, 12, 12, 8, 8, 3, 3, 15, 15, 7, 7, 15, 15, 7, 7, 3, 3)
    ]
    hbm = pl.BlockSpec(memory_space=pltpu.HBM)
    given = (volumes.reshape(4, cells), w_first, w_second, cotangent.reshape(16, cells))
    given = [pltpu.with_memory_space_constraint(a, pltpu.HBM) for a in given]
    vmem = pl.BlockSpec(memory_space=pltpu.VMEM)
    parts = pl.pallas_call(
        functools.partial(kernel, scale),
        out_shape=(
            jax.ShapeDtypeStruct((16, cells), BF16),
            jax.ShapeDtypeStruct((4, cells), BF16),
            jax.ShapeDtypeStruct((8, 1728), F32),
            jax.ShapeDtypeStruct((32, 16, 128), BF16),
        ),
        in_specs=[hbm] * 4,
        out_specs=(vmem,) * 4,
        scratch_shapes=scratch,
        compiler_params=pltpu.CompilerParams(
            collective_id=0, has_side_effects=True, vmem_limit_bytes=48 * 1024 * 1024
        ),
    )(*given)
    feat, ig, g1, g2 = pl.pallas_call(
        finish,
        out_shape=(
            jax.ShapeDtypeStruct((16, cells), BF16),
            jax.ShapeDtypeStruct((4, cells), BF16),
            jax.ShapeDtypeStruct((8, 1728), F32),
            jax.ShapeDtypeStruct((16, 3456), F32),
        ),
        in_specs=[vmem] * 4,
        out_specs=(vmem,) * 4,
        compiler_params=pltpu.CompilerParams(vmem_limit_bytes=8 * 1024 * 1024),
    )(*parts)
    return feat.reshape(16, 1, cells), ig.reshape(4, 1, cells), g1, g2


def solution(mesh):
    return jax.shard_map(
        local_step,
        mesh=mesh,
        in_specs=(P("mp", "sample", None), P("mp", None), P("mp", None), P("mp", "sample", None)),
        out_specs=(P("mp", "sample", None), P("mp", "sample", None), P("mp", None), P("mp", None)),
        check_vma=False,
    )
```
